32 devices in a mesh: dp: 4 (over x, core), ctx: 2 (over y), tensor: 4 (over z).
Axes of the slice: x: 2, y: 2, z: 4, core: 2. Of those that a mesh axis runs over, the one named last changes fastest.
Arguments:
- hidden_in: bfloat16 [8, 1024, 2048], P('dp', 'ctx'), may hold values from -36.5 to 36.5
- lengths: int32 [8], replicated, may hold values from 256 to 1024, as said below
- w_query: bfloat16 [2048, 2048], P(('dp', 'ctx'), 'tensor'), may hold values from -0.125 to 0.125
- w_keyval: bfloat16 [2048, 4, 128], P(('dp', 'ctx'), 'tensor'), may hold values from -0.125 to 0.125
- w_output: bfloat16 [2048, 2048], P(('dp', 'ctx'), 'tensor'), may hold values from -1.5 to 1.5
- w_gateup: bfloat16 [2048, 2, 5632], P(('dp', 'ctx'), None, 'tensor'), may hold values from -0.125 to 0.125
- w_down: bfloat16 [2048, 5632], P(('dp', 'ctx'), 'tensor'), may hold values from -0.078125 to 0.078125
- gain_attn: bfloat16 [2048], P(('dp', 'ctx')), may hold values from 0.5 to 1.5
- gain_mlp: bfloat16 [2048], P(('dp', 'ctx')), may hold values from 0.5 to 1.5
- cotangent: bfloat16 [8, 1024, 2048], P('dp', 'ctx'), may hold values from -6 to 6
Outputs:
- output: bfloat16 [8, 1024, 2048], P('dp', 'ctx')
- input_grad: bfloat16 [8, 1024, 2048], P('dp', 'ctx')
- grad_query: float32 [2048, 2048], P(('dp', 'ctx'), 'tensor')
- grad_keyval: float32 [2048, 4, 128], P(('dp', 'ctx'), 'tensor')
- grad_output: float32 [2048, 2048], P(('dp', 'ctx'), 'tensor')
- grad_gateup: float32 [2048, 2, 5632], P(('dp', 'ctx'), None, 'tensor')
- grad_down: float32 [2048, 5632], P(('dp', 'ctx'), 'tensor')
- grad_gain_attn: float32 [2048], P(('dp', 'ctx'))
- grad_gain_mlp: float32 [2048], P(('dp', 'ctx'))
- root_means: float32 [3], replicated
The draws below stay inside these ranges and needn't reach their ends.
Inputs may be any that keep to these rules, and one draw needn't show every extreme that they name: `lengths`: in every draw the first slot has exactly 1024 valid tokens and the last exactly 256.
All inputs are finite; a program needn't handle non-finite values.
Results may differ from the reference program's by a relative error of at most 0.014.
Values may be sent and summed in bfloat16 or wider, within the bound.
No kernel may reach another device: no remote copies, remote signals or barrier semaphores. Data moves between devices by JAX's collectives and lax.ppermute only.
A program may use at most 384 MiB of HBM per device.

```python
import jax
import jax.numpy as jnp
from jax import lax

D = 2048
HQ = 32
KV = 4
HD = 64
FF = 5632
SEQ = 1024
SLOTS = 8


def draw_lengths(key, part):
    slot_ids = jnp.arange(SLOTS, dtype=jnp.int32)
    base = SEQ - (SEQ - SEQ // 4) * slot_ids // (SLOTS - 1)
    jitter = jax.random.randint(key, (SLOTS,), 0, SEQ // 8 + 1)
    jitter = jnp.where((slot_ids == 0) | (slot_ids == SLOTS - 1), 0, jitter)
    drawn = jnp.maximum(base - jitter, SEQ // 4)
    return drawn.astype(jnp.int32)


def draw_hidden_in(key, part):
    first, second, third = jax.random.split(key, 3)
    fraction = (SLOTS - 1 - jnp.arange(SLOTS, dtype=jnp.float32)) / (SLOTS - 1)
    wobble = jax.random.uniform(first, (SLOTS,), jnp.float32, 0.9, 1.1)
    scales = (0.3 * jnp.exp(fraction * jnp.log(22.0 / 3.0)) * wobble)[:, None, None]
    ranks = jax.random.permutation(third, D)
    channel = jnp.where(ranks < max(D // 128, 2), 6.0, 1.0).astype(jnp.float32)[None, None, :]
    base = jnp.clip(jax.random.normal(second, (SLOTS, SEQ, D), jnp.float32), -2.5, 2.5)
    return (base * scales * channel).astype(jnp.bfloat16)


def levels(stream_key, shape, pieces, low, top_value):
    def one(dim, blocks):
        heights = jax.random.uniform(jax.random.fold_in(jax.random.fold_in(stream_key, 6), dim), (blocks,), jnp.float32, low / len(pieces), top_value / len(pieces))
        return jnp.repeat(jnp.exp(heights), shape[dim] // blocks).reshape((-1,) + (1,) * (len(shape) - dim - 1))

    loudness = one(*pieces[0])
    for cut in pieces[1:]:
        loudness = loudness * one(*cut)
    return loudness


def normal_values(key, dims, scale, reach, cuts=(), held_as=jnp.bfloat16):
    values = jax.random.normal(key, dims, jnp.float32) * scale
    if len(cuts) > 0:
        values = levels(key, dims, cuts, -0.22, 0.18) * values
    return jnp.clip(values, min=-reach, max=reach).astype(held_as)


def setup_inputs(seed: int = 0) -> dict:
    streams_of = jax.random.split(jax.random.key(seed), 11)
    hidden_in = draw_hidden_in(jax.random.fold_in(streams_of[10], 71), 0)
    lengths = draw_lengths(jax.random.fold_in(streams_of[10], 71), 0)
    w_query = normal_values(streams_of[2], (D, HQ * HD), D ** -0.5, 0.125, ((0, 8), (1, 4)))
    w_keyval = normal_values(streams_of[3], (D, KV, 2 * HD), D ** -0.5, 0.125, ((0, 8), (1, 4)))
    w_output = normal_values(streams_of[4], (D, HQ * HD), (HQ * HD // 128) ** -0.5, 1.5, ((0, 8), (1, 4)))
    w_gateup = normal_values(streams_of[5], (D, 2, FF), D ** -0.5, 0.125, ((0, 8), (2, 4)))
    w_down = normal_values(streams_of[6], (D, FF), FF ** -0.5, 0.078125, ((0, 8), (1, 4)))
    gain_attn = jnp.clip(1.0 + 0.1 * jax.random.normal(streams_of[7], (D,), jnp.float32), 0.5, 1.5).astype(jnp.bfloat16)
    gain_mlp = jnp.clip(1.0 + 0.1 * jax.random.normal(streams_of[8], (D,), jnp.float32), 0.5, 1.5).astype(jnp.bfloat16)
    cotangent = normal_values(streams_of[9], (SLOTS, SEQ, D), 1.0, 6.0, ((0, 4), (1, 2)))
    return {"hidden_in": hidden_in, "lengths": lengths, "w_query": w_query, "w_keyval": w_keyval, "w_output": w_output, "w_gateup": w_gateup, "w_down": w_down, "gain_attn": gain_attn, "gain_mlp": gain_mlp, "cotangent": cotangent}


EPS = 1e-05
THETA = 10000.0
NEG_FILL = -1e+30

@jax.custom_vjp
def low(v):
    return lax.optimization_barrier(v.astype(jnp.bfloat16)).astype(jnp.float32)

@jax.custom_vjp
def low_back(v):
    return v

def low_keep(v):
    return (low(v), None)

def low_pass(kept, grad):
    return (grad,)

def back_keep(v):
    return (v, None)

def back_low(kept, grad):
    return (low(grad),)
low.defvjp(low_keep, low_pass)
low_back.defvjp(back_keep, back_low)

def product(left, right):
    return jnp.dot(left, right, precision=lax.Precision.HIGHEST)

def product_cols(left, right):
    return lax.dot_general(left, right, (((1,), (1,)), ((), ())), precision=lax.Precision.HIGHEST)

def rms_norm(values, gain):
    scale = lax.rsqrt(lax.optimization_barrier(jnp.mean(values * values, axis=-1, keepdims=True)) + EPS)
    return values * scale * gain

def rope_tables(positions, head_width):
    frequency = THETA ** (-jnp.arange(0, head_width, 2).astype(jnp.float32) / head_width)
    angles = positions.astype(jnp.float32)[:, None] * frequency[None, :]
    angles = jnp.concatenate([angles, angles], axis=-1)
    return (jnp.cos(angles), jnp.sin(angles))

def rotate(values, cosine, sine):
    half_width = values.shape[-1] // 2
    turned = jnp.concatenate([-values[..., half_width:], values[..., :half_width]], axis=-1)
    return values * cosine + turned * sine

def layer(tokens, length, params):
    query_w, keyval_w, output_w, gateup_w, down_w, attn_gain, mlp_gain = params
    positions = jnp.arange(SEQ, dtype=jnp.int32)
    live_mask = (positions < length).astype(jnp.float32)[:, None]
    cosine, sine = rope_tables(positions, HD)
    normed = low(rms_norm(tokens, attn_gain))
    query_lin = low_back(product(normed, query_w)).reshape(SEQ, HQ, HD)
    keyval_lin = low_back(product(normed, keyval_w.reshape(D, KV * 2 * HD))).reshape(SEQ, KV, 2 * HD)
    queries = low(rotate(query_lin, cosine[:, None, :], sine[:, None, :]))
    keys = low(rotate(keyval_lin[..., :HD], cosine[:, None, :], sine[:, None, :]))
    values = low(keyval_lin[..., HD:])
    grouped = queries.reshape(SEQ, KV, HQ // KV, HD)
    raw_scores = low_back(jnp.einsum('tkgd,ukd->kgtu', grouped, keys, precision=lax.Precision.HIGHEST))
    allowed = (positions[None, :] <= positions[:, None]) & (positions[None, :] < length)
    scores = jnp.where(allowed, raw_scores * HD ** (-0.5), NEG_FILL)
    attend = low(jax.nn.softmax(scores, axis=-1))
    context = jnp.einsum('kgtu,ukd->tkgd', attend, values, precision=lax.Precision.HIGHEST).reshape(SEQ, HQ * HD)
    context = low(low_back(context))
    attn_out = low_back(product_cols(context, output_w))
    middle = tokens + attn_out
    normed_mlp = low(rms_norm(middle, mlp_gain))
    gateup = low_back(product(normed_mlp, gateup_w.reshape(D, 2 * FF))).reshape(SEQ, 2, FF)
    hidden = low(jax.nn.silu(gateup[:, 0]) * gateup[:, 1])
    mlp_out = low_back(product_cols(hidden, down_w))
    result = (middle + mlp_out) * live_mask
    return (result, attn_out, mlp_out, live_mask)

def reference(hidden_in, lengths, w_query, w_keyval, w_output, w_gateup, w_down, gain_attn, gain_mlp, cotangent):
    weights = tuple((entry.astype(jnp.float32) for entry in (w_query, w_keyval, w_output, w_gateup, w_down, gain_attn, gain_mlp)))

    def forward(tokens, *params):

        def one_slot(packed):
            slot_tokens, length = packed
            result, attn_out, mlp_out, live_mask = layer(slot_tokens, length, params)
            squares = jnp.stack([jnp.sum(result * result), jnp.sum(attn_out * attn_out * live_mask), jnp.sum(mlp_out * mlp_out * live_mask)])
            return (result, squares)
        results, squares = lax.map(jax.checkpoint(one_slot), (tokens, lengths))
        return (results, lax.optimization_barrier(jnp.sum(squares, axis=0)))
    results, pullback, square_totals = jax.vjp(forward, hidden_in.astype(jnp.float32), *weights, has_aux=True)
    grads = pullback(cotangent.astype(jnp.float32))
    valid_count = jnp.sum(lengths).astype(jnp.float32) * D
    root_means = jnp.sqrt(square_totals / valid_count)
    return (results.astype(jnp.bfloat16), grads[0].astype(jnp.bfloat16), grads[1], grads[2], grads[3], grads[4], grads[5], grads[6], grads[7], root_means)
```

```python
import functools

import jax
import jax.numpy as jnp
from jax import lax
from jax.experimental import pallas as pl
from jax.experimental.pallas import tpu as pltpu
from jax.sharding import PartitionSpec as P

HD = 64
EPS = 1e-05
THETA = 10000.0
NEG_FILL = -1e30
SLOT_STEP = 1 << 16
NEVER = 1 << 30
BQ = 256
BK = 256
F32 = jnp.float32
BF16 = jnp.bfloat16
ROW_AXES = ("dp", "ctx")


def dot(left, right, left_dim, right_dim):
    return lax.dot_general(
        left, right, (((left_dim,), (right_dim,)), ((), ())), preferred_element_type=F32
    )


def rms_scale(values):
    return lax.rsqrt(jnp.mean(values * values, axis=-1, keepdims=True) + EPS)


def mask_bias(key_code, query_info):
    code, start = query_info[0:1, :], query_info[1:2, :]
    allowed = (key_code <= code) & (key_code >= start)
    return jnp.where(allowed, 0.0, NEG_FILL)


def attend_kernel(heads, blocks, flags, q_ref, info_ref, k_ref, vt_ref, code_ref, o_ref, lse_ref, m_ref, l_ref, acc_ref):
    m_ref[...] = jnp.full_like(m_ref, NEG_FILL)
    l_ref[...] = jnp.zeros_like(l_ref)
    acc_ref[...] = jnp.zeros_like(acc_ref)
    row = pl.program_id(0)

    def step(kb, carry):
        @pl.when(flags[row * blocks + kb] > 0)
        def _():
            at = pl.multiple_of(kb * BK, BK)
            keys = k_ref[pl.ds(at, BK), :]
            values_t = vt_ref[:, pl.ds(at, BK)]
            bias = mask_bias(code_ref[pl.ds(at, BK), :], info_ref[...])
            for h in range(heads):
                part = slice(h * HD, (h + 1) * HD)
                scores = dot(keys, q_ref[part, :], 1, 0) + bias
                before = m_ref[h : h + 1, :]
                top = jnp.maximum(before, jnp.max(scores, axis=0, keepdims=True))
                shrink = jnp.exp(before - top)
                weights = jnp.exp(scores - top)
                l_ref[h : h + 1, :] = shrink * l_ref[h : h + 1, :] + jnp.sum(weights, axis=0, keepdims=True)
                acc_ref[part, :] = shrink * acc_ref[part, :] + dot(values_t, weights.astype(BF16), 1, 0)
                m_ref[h : h + 1, :] = top

        return carry

    lax.fori_loop(0, blocks, step, 0)
    total = l_ref[...]
    total = jnp.where(total == 0.0, 1.0, total)
    lse_ref[...] = m_ref[...] + jnp.log(total)
    for h in range(heads):
        part = slice(h * HD, (h + 1) * HD)
        o_ref[part, :] = (acc_ref[part, :] / total[h : h + 1, :]).astype(BF16)


def attend(flags, q_t, info, keys, values_t, codes):
    width, rows = q_t.shape
    heads = width // HD
    count = keys.shape[0]
    blocks = count // BK
    whole = lambda i, f: (0, 0)
    column = lambda i, f: (0, i)
    return pl.pallas_call(
        functools.partial(attend_kernel, heads, blocks),
        out_shape=(
            jax.ShapeDtypeStruct((width, rows), BF16),
            jax.ShapeDtypeStruct((heads, rows), F32),
        ),
        grid_spec=pltpu.PrefetchScalarGridSpec(
            num_scalar_prefetch=1,
            grid=(rows // BQ,),
            in_specs=[
                pl.BlockSpec((width, BQ), column),
                pl.BlockSpec((2, BQ), column),
                pl.BlockSpec((count, HD), whole),
                pl.BlockSpec((HD, count), whole),
                pl.BlockSpec((count, 1), whole),
            ],
            out_specs=[pl.BlockSpec((width, BQ), column), pl.BlockSpec((heads, BQ), column)],
            scratch_shapes=[
                pltpu.VMEM((heads, BQ), F32),
                pltpu.VMEM((heads, BQ), F32),
                pltpu.VMEM((width, BQ), F32),
            ],
        ),
        compiler_params=pltpu.CompilerParams(vmem_limit_bytes=24 << 20),
        cost_estimate=pl.CostEstimate(
            flops=8 * rows * count * width, bytes_accessed=4 * rows * width, transcendentals=0
        ),
        name="attend",
    )(flags, q_t, info, keys, values_t, codes)


def attend_back_kernel(
    heads, blocks, flags, q_ref, do_ref, o_ref, lse_ref, info_ref, cos_ref, sin_ref, k_ref, v_ref, kt_ref, code_ref,
    dq_ref, dk_ref, dv_ref, acc_ref, delta_ref,
):
    row = pl.program_id(0)

    @pl.when(row == 0)
    def _():
        dk_ref[...] = jnp.zeros_like(dk_ref)
        dv_ref[...] = jnp.zeros_like(dv_ref)

    acc_ref[...] = jnp.zeros_like(acc_ref)
    for h in range(heads):
        part = slice(h * HD, (h + 1) * HD)
        delta_ref[h : h + 1, :] = jnp.sum(
            do_ref[part, :].astype(F32) * o_ref[part, :].astype(F32), axis=0, keepdims=True
        )

    def step(kb, carry):
        @pl.when(flags[row * blocks + kb] > 0)
        def _():
            at = pl.multiple_of(kb * BK, BK)
            keys = k_ref[pl.ds(at, BK), :]
            values = v_ref[pl.ds(at, BK), :]
            keys_t = kt_ref[:, pl.ds(at, BK)]
            bias = mask_bias(code_ref[pl.ds(at, BK), :], info_ref[...])
            grad_keys = jnp.zeros((BK, HD), F32)
            grad_values = jnp.zeros((BK, HD), F32)
            for h in range(heads):
                part = slice(h * HD, (h + 1) * HD)
                queries = q_ref[part, :]
                grads = do_ref[part, :]
                weights = jnp.exp(dot(keys, queries, 1, 0) + bias - lse_ref[h : h + 1, :])
                grad_weights = dot(values, grads, 1, 0)
                raw = (weights * (grad_weights - delta_ref[h : h + 1, :])).astype(BF16)
                grad_values = grad_values + dot(weights.astype(BF16), grads, 1, 1)
                grad_keys = grad_keys + dot(raw, queries, 1, 1)
                acc_ref[part, :] += dot(keys_t, raw, 1, 0)
            dk_ref[pl.ds(at, BK), :] += grad_keys
            dv_ref[pl.ds(at, BK), :] += grad_values

        return carry

    lax.fori_loop(0, blocks, step, 0)
    cosine, sine = cos_ref[...], sin_ref[...]
    half = HD // 2
    for h in range(heads):
        lower = acc_ref[h * HD : h * HD + half, :] * HD**-0.5
        upper = acc_ref[h * HD + half : (h + 1) * HD, :] * HD**-0.5
        dq_ref[h * HD : h * HD + half, :] = (lower * cosine + upper * sine).astype(BF16)
        dq_ref[h * HD + half : (h + 1) * HD, :] = (upper * cosine - lower * sine).astype(BF16)


def attend_back(flags, q_t, grad_t, o_t, lse, info, cosine_t, sine_t, keys, values, keys_t, codes):
    width, rows = q_t.shape
    heads = width // HD
    count = keys.shape[0]
    blocks = count // BK
    whole = lambda i, f: (0, 0)
    column = lambda i, f: (0, i)
    return pl.pallas_call(
        functools.partial(attend_back_kernel, heads, blocks),
        out_shape=(
            jax.ShapeDtypeStruct((width, rows), BF16),
            jax.ShapeDtypeStruct((count, HD), F32),
            jax.ShapeDtypeStruct((count, HD), F32),
        ),
        grid_spec=pltpu.PrefetchScalarGridSpec(
            num_scalar_prefetch=1,
            grid=(rows // BQ,),
            in_specs=[
                pl.BlockSpec((width, BQ), column),
                pl.BlockSpec((width, BQ), column),
                pl.BlockSpec((width, BQ), column),
                pl.BlockSpec((heads, BQ), column),
                pl.BlockSpec((2, BQ), column),
                pl.BlockSpec((HD // 2, BQ), column),
                pl.BlockSpec((HD // 2, BQ), column),
                pl.BlockSpec((count, HD), whole),
                pl.BlockSpec((count, HD), whole),
                pl.BlockSpec((HD, count), whole),
                pl.BlockSpec((count, 1), whole),
            ],
            out_specs=[
                pl.BlockSpec((width, BQ), column),
                pl.BlockSpec((count, HD), whole),
                pl.BlockSpec((count, HD), whole),
            ],
            scratch_shapes=[pltpu.VMEM((width, BQ), F32), pltpu.VMEM((heads, BQ), F32)],
        ),
        compiler_params=pltpu.CompilerParams(vmem_limit_bytes=32 << 20),
        cost_estimate=pl.CostEstimate(
            flops=20 * rows * count * width, bytes_accessed=8 * rows * width, transcendentals=0
        ),
        name="attend_back",
    )(flags, q_t, grad_t, o_t, lse, info, cosine_t, sine_t, keys, values, keys_t, codes)


def block_flags(codes, starts, key_codes):
    top = jnp.max(codes.reshape(-1, BQ), axis=1)
    low = jnp.min(starts.reshape(-1, BQ), axis=1)
    blocks = key_codes.reshape(-1, BK)
    key_low = jnp.min(blocks, axis=1)
    key_top = jnp.max(jnp.where(blocks < NEVER, blocks, -1), axis=1)
    seen = (key_low[None, :] <= top[:, None]) & (key_top[None, :] >= low[:, None])
    return seen.astype(jnp.int32).reshape(-1)


def chain_sum(part):
    place = lax.axis_index("tensor")
    inner = (place == 1) | (place == 2)
    first = lax.ppermute(part, "tensor", [(0, 1), (3, 2)])
    pair = lax.optimization_barrier((part.astype(F32) + first.astype(F32)).astype(BF16))
    second = lax.ppermute(pair, "tensor", [(1, 2), (2, 1)])
    total = lax.optimization_barrier((pair.astype(F32) + second.astype(F32)).astype(BF16))
    third = lax.ppermute(total, "tensor", [(1, 0), (2, 3)])
    return lax.optimization_barrier(jnp.where(inner, total, third))


def gather_rows(shard):
    return lax.all_gather(shard, ROW_AXES, axis=0, tiled=True)


def scatter_rows(grads):
    return lax.psum_scatter(grads, ROW_AXES, scatter_dimension=0, tiled=True).astype(F32)


def body(hidden_in, lengths, w_query, w_keyval, w_output, w_gateup, w_down, gain_attn, gain_mlp, cotangent):
    micro, span, width = hidden_in.shape
    rows = micro * span
    shard_rows = w_query.shape[0]
    q_width = w_query.shape[1]
    ff = w_down.shape[1]
    heads = q_width // HD
    half = HD // 2
    here = lax.axis_index("ctx")

    gains = jnp.stack([gain_attn, gain_mlp], axis=1)
    gains = jnp.pad(gains, ((0, 0), (0, 126)))
    packed = jnp.concatenate([w_query, w_keyval.reshape(shard_rows, -1), gains], axis=1)
    first = gather_rows(packed)
    qkv_w = first[:, : q_width + 2 * HD]
    gain_pair = first[:, q_width + 2 * HD : q_width + 2 * HD + 2].astype(F32).T
    attn_gain, mlp_gain = gain_pair[0:1], gain_pair[1:2]
    output_w = gather_rows(w_output)
    gateup_w = gather_rows(w_gateup.reshape(shard_rows, 2 * ff))
    down_w = gather_rows(w_down)

    slot_lengths = lax.dynamic_slice_in_dim(lengths, lax.axis_index("dp") * micro, micro)
    slot_of = jnp.repeat(jnp.arange(micro, dtype=jnp.int32), span)
    length_of = jnp.repeat(slot_lengths, span)
    offset = jnp.tile(jnp.arange(span, dtype=jnp.int32), micro)
    position = here * span + offset
    other_position = (1 - here) * span + offset
    live = (position < length_of).astype(F32)[:, None]
    starts = slot_of * SLOT_STEP
    codes = starts + position
    own_codes = jnp.where(position < length_of, codes, NEVER)
    other_codes = jnp.where(other_position < length_of, starts + other_position, NEVER)
    key_codes = jnp.concatenate([own_codes, other_codes])
    info = jnp.stack([codes, starts])
    flags = block_flags(codes, starts, key_codes)
    key_codes = key_codes[:, None]

    frequency = THETA ** (-jnp.arange(0, HD, 2).astype(F32) / HD)
    angles = position.astype(F32)[:, None] * frequency[None, :]
    cosine, sine = jnp.cos(angles), jnp.sin(angles)
    cosine_t, sine_t = cosine.T, sine.T

    hidden_flat = hidden_in.reshape(rows, width)
    tokens = hidden_flat.astype(F32)
    seed_flat = cotangent.reshape(rows, width)

    attn_scale = rms_scale(tokens)
    normed = (tokens * attn_scale * attn_gain).astype(BF16)
    q_lin = dot(qkv_w[:, :q_width], normed, 0, 1).reshape(heads, 2, half, rows) * HD**-0.5
    q_t = jnp.stack(
        [
            q_lin[:, 0] * cosine_t - q_lin[:, 1] * sine_t,
            q_lin[:, 1] * cosine_t + q_lin[:, 0] * sine_t,
        ],
        axis=1,
    ).astype(BF16).reshape(q_width, rows)
    kv_lin = dot(normed, qkv_w[:, q_width:], 1, 0)
    k_low, k_high = kv_lin[:, :half], kv_lin[:, half:HD]
    own_pair = jnp.concatenate(
        [k_low * cosine - k_high * sine, k_high * cosine + k_low * sine, kv_lin[:, HD:]], axis=1
    ).astype(BF16)
    other_pair = lax.ppermute(own_pair, "ctx", [(0, 1), (1, 0)])
    pairs = jnp.concatenate([own_pair, other_pair], axis=0)
    pairs_t = pairs.T
    keys, values = pairs[:, :HD], pairs[:, HD:]
    keys_t, values_t = pairs_t[:HD], pairs_t[HD:]
    chunks = [(m * span, span) for m in range(micro)]
    blocks = span // BQ

    context_t, lse = [], []
    flag_blocks = key_codes.shape[0] // BK
    for m in range(micro):
        lo = m * span
        one_flags = flags[m * blocks * flag_blocks : (m + 1) * blocks * flag_blocks]
        got = attend(one_flags, q_t[:, lo : lo + span], info[:, lo : lo + span], keys, values_t, key_codes)
        context_t.append(got[0])
        lse.append(got[1])
    attn_out, middle, mlp_scale, normed_mlp = [], [], [], []
    hidden, grad_gateup, mlp_out, grad_normed_mlp = [], [], [], []
    for m, (lo, size) in enumerate(chunks):
        part = dot(context_t[m], output_w, 0, 1).astype(BF16)
        attn_out.append(chain_sum(part).astype(F32))
        middle.append(tokens[lo : lo + size] + attn_out[m])
        mlp_scale.append(rms_scale(middle[m]))
        normed_mlp.append((middle[m] * mlp_scale[m] * mlp_gain).astype(BF16))

    seeds = [seed_flat[lo : lo + size].astype(F32) * live[lo : lo + size] for lo, size in chunks]
    for m, (lo, size) in enumerate(chunks):
        mlp_seed = seeds[m].astype(BF16)
        grad_hidden = dot(mlp_seed, down_w, 1, 0)
        gateup = dot(normed_mlp[m], gateup_w, 1, 0)
        gate, up = gateup[:, :ff], gateup[:, ff:]
        sigma = jax.nn.sigmoid(gate)
        activated = gate * sigma
        hidden.append((activated * up).astype(BF16))
        grad_gate = grad_hidden * up * (sigma * (1.0 + gate * (1.0 - sigma)))
        grad_gateup.append(jnp.concatenate([grad_gate, grad_hidden * activated], axis=1).astype(BF16))
        back = dot(grad_gateup[m], gateup_w, 1, 1).astype(BF16)
        grad_normed_mlp.append(chain_sum(back).astype(F32))
    for m in range(micro):
        mlp_out.append(chain_sum(dot(hidden[m], down_w, 1, 1).astype(BF16)).astype(F32))

    grad_middle, attn_seed, grad_q_t = [], [], []
    gain_mlp_sum = 0.0
    grad_keys, grad_values = 0.0, 0.0
    for m, (lo, size) in enumerate(chunks):
        weighted = grad_normed_mlp[m] * mlp_gain
        scale = mlp_scale[m]
        grad_middle.append(
            seeds[m] + scale * weighted - middle[m] * scale**3 * jnp.mean(weighted * middle[m], axis=-1, keepdims=True)
        )
        gain_mlp_sum = gain_mlp_sum + jnp.sum(grad_normed_mlp[m] * middle[m] * scale, axis=0)
        attn_seed.append(grad_middle[m].astype(BF16))
        grad_context_t = dot(output_w, attn_seed[m], 0, 1).astype(BF16)
        one_flags = flags[m * blocks * flag_blocks : (m + 1) * blocks * flag_blocks]
        got = attend_back(
            one_flags,
            q_t[:, lo : lo + size],
            grad_context_t,
            context_t[m],
            lse[m],
            info[:, lo : lo + size],
            cosine_t[:, lo : lo + size],
            sine_t[:, lo : lo + size],
            keys,
            values,
            keys_t,
            key_codes,
        )
        grad_q_t.append(got[0])
        grad_keys = grad_keys + got[1]
        grad_values = grad_values + got[2]
    sent = jnp.concatenate([grad_keys[rows:], grad_values[rows:]], axis=1)
    returned = lax.ppermute(sent, "ctx", [(0, 1), (1, 0)])
    own_keys = grad_keys[:rows] + returned[:, :HD]
    own_values = grad_values[:rows] + returned[:, HD:]
    low, high = own_keys[:, :half], own_keys[:, half:]
    grad_pair = jnp.concatenate([low * cosine + high * sine, high * cosine - low * sine, own_values], axis=1)
    grad_pair_t = grad_pair.astype(BF16).T
    grad_qkv_t = jnp.concatenate([jnp.concatenate(grad_q_t, axis=1), grad_pair_t], axis=0)
    input_grad = []
    gain_attn_sum = 0.0
    for m, (lo, size) in enumerate(chunks):
        back = dot(grad_qkv_t[:, lo : lo + size], qkv_w, 0, 1)
        grad_normed = chain_sum(back.astype(BF16)).astype(F32)
        one = tokens[lo : lo + size]
        scale = attn_scale[lo : lo + size]
        weighted = grad_normed * attn_gain
        input_grad.append(
            (grad_middle[m] + scale * weighted - one * scale**3 * jnp.mean(weighted * one, axis=-1, keepdims=True)).astype(BF16)
        )
        gain_attn_sum = gain_attn_sum + jnp.sum(grad_normed * one * scale, axis=0)

    output, squares = [], jnp.zeros((3,), F32)
    for m, (lo, size) in enumerate(chunks):
        alive = live[lo : lo + size]
        result = (middle[m] + mlp_out[m]) * alive
        output.append(result.astype(BF16))
        squares = squares + jnp.stack(
            [jnp.sum(result * result), jnp.sum(attn_out[m] ** 2 * alive), jnp.sum(mlp_out[m] ** 2 * alive)]
        )

    join = lambda parts: jnp.concatenate(parts, axis=0)
    mlp_seed = join(seeds).astype(BF16)
    grad_down = scatter_rows(dot(mlp_seed, join(hidden), 0, 0).astype(BF16))
    grad_gateup_w = scatter_rows(dot(join(normed_mlp), join(grad_gateup), 0, 0).astype(BF16))
    grad_output = scatter_rows(dot(join(attn_seed), jnp.concatenate(context_t, axis=1), 0, 1).astype(BF16))
    grad_qkv = scatter_rows(dot(normed, grad_qkv_t, 0, 1).astype(BF16))

    small = jnp.concatenate([gain_attn_sum, gain_mlp_sum, squares])
    small = lax.psum(small, ROW_AXES)
    valid_count = jnp.sum(lengths).astype(F32) * width
    root_means = jnp.sqrt(small[2 * width :] / valid_count)
    shard = (lax.axis_index("dp") * lax.axis_size("ctx") + here) * shard_rows
    return (
        join(output).reshape(hidden_in.shape),
        join(input_grad).reshape(hidden_in.shape),
        grad_qkv[:, :q_width],
        grad_qkv[:, q_width:].reshape(w_keyval.shape),
        grad_output,
        grad_gateup_w.reshape(w_gateup.shape),
        grad_down,
        lax.dynamic_slice_in_dim(small, shard, shard_rows),
        lax.dynamic_slice_in_dim(small, width + shard, shard_rows),
        root_means,
    )


def solution(mesh):
    placed = (
        P("dp", "ctx", None),
        P(),
        P(("dp", "ctx"), "tensor"),
        P(("dp", "ctx"), "tensor", None),
        P(("dp", "ctx"), "tensor"),
        P(("dp", "ctx"), None, "tensor"),
        P(("dp", "ctx"), "tensor"),
        P(("dp", "ctx")),
        P(("dp", "ctx")),
        P("dp", "ctx", None),
    )
    return jax.shard_map(
        body,
        mesh=mesh,
        in_specs=placed,
        out_specs=(
            P("dp", "ctx", None),
            P("dp", "ctx", None),
            P(("dp", "ctx"), "tensor"),
            P(("dp", "ctx"), "tensor", None),
            P(("dp", "ctx"), "tensor"),
            P(("dp", "ctx"), None, "tensor"),
            P(("dp", "ctx"), "tensor"),
            P(("dp", "ctx")),
            P(("dp", "ctx")),
            P(),
        ),
        check_vma=False,
    )
```

```python
import functools

import jax
import jax.numpy as jnp
from jax import lax
from jax.experimental import pallas as pl
from jax.experimental.pallas import tpu as pltpu
from jax.sharding import PartitionSpec as P

HD = 64
EPS = 1e-05
THETA = 10000.0
NEG_FILL = -1e30
SLOT_STEP = 1 << 16
NEVER = 1 << 30
BQ = 256
BK = 256
SIDE = 1
F32 = jnp.float32
BF16 = jnp.bfloat16
SMALL_COST = pl.CostEstimate(flops=1024, bytes_accessed=1024, transcendentals=0)
ROW_AXES = ("dp", "ctx")


def dot(left, right, left_dim, right_dim):
    return lax.dot_general(
        left, right, (((left_dim,), (right_dim,)), ((), ())), preferred_element_type=F32
    )


def rms_scale(values):
    return lax.rsqrt(jnp.mean(values * values, axis=-1, keepdims=True) + EPS)


def mask_bias(key_code, query_info):
    code, start = query_info[0:1, :], query_info[1:2, :]
    allowed = (key_code <= code) & (key_code >= start)
    return jnp.where(allowed, 0.0, NEG_FILL)


def beside(parts):
    return jnp.concatenate(parts, axis=1)


def heads_of(ref, rows):
    return beside([ref[r * HD : (r + 1) * HD, :] for r in rows])


def rows_of(ref, rows):
    return beside([ref[r : r + 1, :] for r in rows])


def attend_kernel(heads, blocks, flags, q_ref, info_ref, k_ref, vt_ref, code_ref, o_ref, lse_ref, m_ref, l_ref, acc_ref):
    m_ref[...] = jnp.full_like(m_ref, NEG_FILL)
    l_ref[...] = jnp.zeros_like(l_ref)
    acc_ref[...] = jnp.zeros_like(acc_ref)
    row = pl.program_id(0)

    def step(kb, carry):
        @pl.when(flags[row * blocks + kb] > 0)
        def _():
            at = pl.multiple_of(kb * BK, BK)
            keys = k_ref[pl.ds(at, BK), :]
            values_t = vt_ref[:, pl.ds(at, BK)]
            bias = beside([mask_bias(code_ref[pl.ds(at, BK), :], info_ref[...])] * SIDE)
            for h in range(0, heads, SIDE):
                rows = range(h, h + SIDE)
                scores = dot(keys, heads_of(q_ref, rows), 1, 0) + bias
                before = rows_of(m_ref, rows)
                top = jnp.maximum(before, jnp.max(scores, axis=0, keepdims=True))
                shrink = jnp.exp(before - top)
                weights = jnp.exp(scores - top)
                total = shrink * rows_of(l_ref, rows) + jnp.sum(weights, axis=0, keepdims=True)
                out = shrink * heads_of(acc_ref, rows) + dot(values_t, weights.astype(BF16), 1, 0)
                for n, r in enumerate(rows):
                    lanes = slice(n * BQ, (n + 1) * BQ)
                    m_ref[r : r + 1, :] = top[:, lanes]
                    l_ref[r : r + 1, :] = total[:, lanes]
                    acc_ref[r * HD : (r + 1) * HD, :] = out[:, lanes]

        return carry

    lax.fori_loop(0, blocks, step, 0)
    total = l_ref[...]
    total = jnp.where(total == 0.0, 1.0, total)
    lse_ref[...] = m_ref[...] + jnp.log(total)
    for h in range(heads):
        part = slice(h * HD, (h + 1) * HD)
        o_ref[part, :] = (acc_ref[part, :] / total[h : h + 1, :]).astype(BF16)


def attend(flags, q_t, info, keys, values_t, codes):
    width, rows = q_t.shape
    heads = width // HD
    count = keys.shape[0]
    blocks = count // BK
    whole = lambda i, f: (0, 0)
    column = lambda i, f: (0, i)
    return pl.pallas_call(
        functools.partial(attend_kernel, heads, blocks),
        out_shape=(
            jax.ShapeDtypeStruct((width, rows), BF16),
            jax.ShapeDtypeStruct((heads, rows), F32),
        ),
        grid_spec=pltpu.PrefetchScalarGridSpec(
            num_scalar_prefetch=1,
            grid=(rows // BQ,),
            in_specs=[
                pl.BlockSpec((width, BQ), column),
                pl.BlockSpec((2, BQ), column),
                pl.BlockSpec((count, HD), whole),
                pl.BlockSpec((HD, count), whole),
                pl.BlockSpec((count, 1), whole),
            ],
            out_specs=[pl.BlockSpec((width, BQ), column), pl.BlockSpec((heads, BQ), column)],
            scratch_shapes=[
                pltpu.VMEM((heads, BQ), F32),
                pltpu.VMEM((heads, BQ), F32),
                pltpu.VMEM((width, BQ), F32),
            ],
        ),
        compiler_params=pltpu.CompilerParams(vmem_limit_bytes=24 << 20),
        cost_estimate=SMALL_COST,
        name="attend",
    )(flags, q_t, info, keys, values_t, codes)


def attend_back_kernel(
    heads, blocks, flags, q_ref, do_ref, o_ref, lse_ref, info_ref, cos_ref, sin_ref, k_ref, v_ref, kt_ref, code_ref,
    dq_ref, dk_ref, dv_ref, acc_ref, delta_ref,
):
    row = pl.program_id(0)

    @pl.when(row == 0)
    def _():
        dk_ref[...] = jnp.zeros_like(dk_ref)
        dv_ref[...] = jnp.zeros_like(dv_ref)

    acc_ref[...] = jnp.zeros_like(acc_ref)
    for h in range(heads):
        part = slice(h * HD, (h + 1) * HD)
        delta_ref[h : h + 1, :] = jnp.sum(
            do_ref[part, :].astype(F32) * o_ref[part, :].astype(F32), axis=0, keepdims=True
        )

    def step(kb, carry):
        @pl.when(flags[row * blocks + kb] > 0)
        def _():
            at = pl.multiple_of(kb * BK, BK)
            keys = k_ref[pl.ds(at, BK), :]
            values = v_ref[pl.ds(at, BK), :]
            keys_t = kt_ref[:, pl.ds(at, BK)]
            bias = beside([mask_bias(code_ref[pl.ds(at, BK), :], info_ref[...])] * SIDE)
            grad_keys = jnp.zeros((BK, HD), F32)
            grad_values = jnp.zeros((BK, HD), F32)
            for h in range(0, heads, SIDE):
                rows = range(h, h + SIDE)
                queries = heads_of(q_ref, rows)
                grads = heads_of(do_ref, rows)
                weights = jnp.exp(dot(keys, queries, 1, 0) + bias - rows_of(lse_ref, rows))
                grad_weights = dot(values, grads, 1, 0)
                raw = (weights * (grad_weights - rows_of(delta_ref, rows))).astype(BF16)
                grad_values = grad_values + dot(weights.astype(BF16), grads, 1, 1)
                grad_keys = grad_keys + dot(raw, queries, 1, 1)
                out = dot(keys_t, raw, 1, 0)
                for n, r in enumerate(rows):
                    acc_ref[r * HD : (r + 1) * HD, :] += out[:, n * BQ : (n + 1) * BQ]
            dk_ref[pl.ds(at, BK), :] += grad_keys
            dv_ref[pl.ds(at, BK), :] += grad_values

        return carry

    lax.fori_loop(0, blocks, step, 0)
    cosine, sine = cos_ref[...], sin_ref[...]
    half = HD // 2
    for h in range(heads):
        lower = acc_ref[h * HD : h * HD + half, :] * HD**-0.5
        upper = acc_ref[h * HD + half : (h + 1) * HD, :] * HD**-0.5
        dq_ref[h * HD : h * HD + half, :] = (lower * cosine + upper * sine).astype(BF16)
        dq_ref[h * HD + half : (h + 1) * HD, :] = (upper * cosine - lower * sine).astype(BF16)


def attend_back(flags, q_t, grad_t, o_t, lse, info, cosine_t, sine_t, keys, values, keys_t, codes):
    width, rows = q_t.shape
    heads = width // HD
    count = keys.shape[0]
    blocks = count // BK
    whole = lambda i, f: (0, 0)
    column = lambda i, f: (0, i)
    return pl.pallas_call(
        functools.partial(attend_back_kernel, heads, blocks),
        out_shape=(
            jax.ShapeDtypeStruct((width, rows), BF16),
            jax.ShapeDtypeStruct((count, HD), F32),
            jax.ShapeDtypeStruct((count, HD), F32),
        ),
        grid_spec=pltpu.PrefetchScalarGridSpec(
            num_scalar_prefetch=1,
            grid=(rows // BQ,),
            in_specs=[
                pl.BlockSpec((width, BQ), column),
                pl.BlockSpec((width, BQ), column),
                pl.BlockSpec((width, BQ), column),
                pl.BlockSpec((heads, BQ), column),
                pl.BlockSpec((2, BQ), column),
                pl.BlockSpec((HD // 2, BQ), column),
                pl.BlockSpec((HD // 2, BQ), column),
                pl.BlockSpec((count, HD), whole),
                pl.BlockSpec((count, HD), whole),
                pl.BlockSpec((HD, count), whole),
                pl.BlockSpec((count, 1), whole),
            ],
            out_specs=[
                pl.BlockSpec((width, BQ), column),
                pl.BlockSpec((count, HD), whole),
                pl.BlockSpec((count, HD), whole),
            ],
            scratch_shapes=[pltpu.VMEM((width, BQ), F32), pltpu.VMEM((heads, BQ), F32)],
        ),
        compiler_params=pltpu.CompilerParams(vmem_limit_bytes=32 << 20),
        cost_estimate=SMALL_COST,
        name="attend_back",
    )(flags, q_t, grad_t, o_t, lse, info, cosine_t, sine_t, keys, values, keys_t, codes)


def block_flags(codes, starts, key_codes):
    top = jnp.max(codes.reshape(-1, BQ), axis=1)
    low = jnp.min(starts.reshape(-1, BQ), axis=1)
    blocks = key_codes.reshape(-1, BK)
    key_low = jnp.min(blocks, axis=1)
    key_top = jnp.max(jnp.where(blocks < NEVER, blocks, -1), axis=1)
    seen = (key_low[None, :] <= top[:, None]) & (key_top[None, :] >= low[:, None])
    return seen.astype(jnp.int32).reshape(-1)


def rowwise_kernel(fn, bounds, lists, flats, consts, outs, choice, *refs):
    pieces = len(bounds)
    n_list = lists * pieces
    step = pl.program_id(0)
    flat_refs = refs[n_list : n_list + flats]
    const_refs = refs[n_list + flats : n_list + flats + consts]
    out_refs = refs[len(refs) - outs[0] - outs[1] : len(refs) - outs[1]]
    sum_refs = refs[len(refs) - outs[1] :]

    if outs[1]:
        @pl.when(step == 0)
        def _():
            for ref in sum_refs:
                ref[...] = jnp.zeros_like(ref)

    for j, (lo, hi) in enumerate(bounds):
        @pl.when((step >= lo) & (step < hi))
        def _():
            got, sums = fn(
                choice[0],
                [refs[k * pieces + j][...].astype(F32) for k in range(lists)],
                [ref[...].astype(F32) for ref in flat_refs],
                [ref[...] for ref in const_refs],
            )
            for ref, value in zip(out_refs, got):
                ref[...] = value.astype(ref.dtype)
            for ref, value in zip(sum_refs, sums):
                ref[...] += value


def tile_of(size):
    return next(tile for tile in (128, 160, 96, 64, 32, 16) if size % tile == 0)


def rowwise(fn, choice, lists, flats, consts, outs, sums=0, after=(), name="rowwise"):
    tile = tile_of(lists[0][0].shape[0])
    sizes = [piece.shape[0] // tile for piece in lists[0]]
    width = lists[0][0].shape[1]
    bounds, lo = [], 0
    for size in sizes:
        bounds.append((lo, lo + size))
        lo += size
    total = lo

    def piece_map(lo, size):
        return lambda i, c: (jnp.clip(i - lo, 0, size - 1), 0)

    in_specs, operands = [], []
    for pieces in lists:
        for piece, (lo, hi) in zip(pieces, bounds):
            in_specs.append(pl.BlockSpec((tile, width), piece_map(lo, hi - lo)))
            operands.append(piece)
    for array, first in flats:
        offset = first // tile
        in_specs.append(pl.BlockSpec((tile, array.shape[1]), lambda i, c, offset=offset: (i + offset, 0)))
        operands.append(array)
    for array in consts:
        in_specs.append(pl.BlockSpec((1, array.shape[1]), lambda i, c: (0, 0)))
        operands.append(array)
    for array in after:
        in_specs.append(pl.BlockSpec(memory_space=pl.ANY))
        operands.append(array)
    rows = total * tile
    return pl.pallas_call(
        functools.partial(rowwise_kernel, fn, bounds, len(lists), len(flats), len(consts), (len(outs), sums)),
        out_shape=[jax.ShapeDtypeStruct((rows, width), dtype) for dtype in outs]
        + [jax.ShapeDtypeStruct((1, width), F32)] * sums,
        grid_spec=pltpu.PrefetchScalarGridSpec(
            num_scalar_prefetch=1,
            grid=(total,),
            in_specs=in_specs,
            out_specs=[pl.BlockSpec((tile, width), lambda i, c: (i, 0))] * len(outs)
            + [pl.BlockSpec((1, width), lambda i, c: (0, 0))] * sums,
        ),
        compiler_params=pltpu.CompilerParams(vmem_limit_bytes=32 << 20),
        cost_estimate=SMALL_COST,
        name=name,
    )(choice, *operands)


def add_fn(choice, lists, flats, consts):
    return [lists[0] + lists[1]], []


def pick(choice, total, third):
    return jnp.where(choice > 0, total, third)


def row_scale(values):
    return lax.rsqrt(jnp.mean(values * values, axis=1, keepdims=True) + EPS)


def middle_fn(choice, lists, flats, consts):
    branch = pick(choice, lists[0], lists[1])
    middle = flats[0] + branch
    return [branch, middle * row_scale(middle) * consts[0]], []


def column_sum(values):
    return jnp.sum(values, axis=0, keepdims=True)


def grad_middle_fn(choice, lists, flats, consts):
    grad = pick(choice, lists[0], lists[1])
    tokens, branch, seed, live = flats
    middle = tokens + branch
    scale = row_scale(middle)
    weighted = grad * consts[0]
    mean = jnp.mean(weighted * middle, axis=1, keepdims=True)
    out = seed * live + scale * weighted - middle * scale**3 * mean
    return [out, out], [column_sum(grad * middle * scale)]


def input_grad_fn(choice, lists, flats, consts):
    grad = pick(choice, lists[0], lists[1])
    tokens, grad_middle = flats
    scale = row_scale(tokens)
    weighted = grad * consts[0]
    mean = jnp.mean(weighted * tokens, axis=1, keepdims=True)
    return [grad_middle + scale * weighted - tokens * scale**3 * mean], []


def result_fn(choice, lists, flats, consts):
    mlp_branch = pick(choice, lists[0], lists[1])
    tokens, branch, live = flats
    result = (tokens + branch + mlp_branch) * live
    return [result], [
        column_sum(result * result),
        column_sum(branch * branch * live),
        column_sum(mlp_branch * mlp_branch * live),
    ]


def send_in(part):
    return lax.ppermute(part, "tensor", [(0, 1), (3, 2)])


def send_across(pair):
    return lax.ppermute(pair, "tensor", [(1, 2), (2, 1)])


def send_out(total):
    return lax.ppermute(total, "tensor", [(1, 0), (2, 3)])


def held_back(value, dep):
    return value + dep[:1, :1].astype(F32) * 0.0


class Sums:
    def __init__(self, choice):
        self.choice = choice
        self.last = None
        self.order = []
        self.parts, self.firsts, self.pairs, self.seconds, self.totals, self.thirds = {}, {}, {}, {}, {}, {}

    def ordered(self, fn, *args, **more):
        after = tuple(more.pop("after", ()))
        if self.last is not None:
            after += (self.last,)
        got = rowwise(fn, self.choice, *args, after=after, **more)
        self.last = got[0]
        return got

    def push(self, k, part):
        self.order.append(k)
        self.parts[k] = part
        self.firsts[k] = send_in(part)

    def pair(self, k, after=()):
        spot = self.order.index(k)
        if spot >= 3:
            after = tuple(after) + (self.thirds[self.order[spot - 3]],)
        both = [[self.parts[k]], [self.firsts[k]]]
        self.pairs[k] = self.ordered(add_fn, both, [], [], [BF16], after=after, name="pair")[0]
        self.seconds[k] = send_across(self.pairs[k])

    def total(self, k, after=()):
        both = [[self.pairs[k]], [self.seconds[k]]]
        self.totals[k] = self.ordered(add_fn, both, [], [], [BF16], after=after, name="total")[0]
        self.thirds[k] = send_out(self.totals[k])

    def of(self, picked):
        return [self.totals[k] for k in picked], [self.thirds[k] for k in picked]


def small_sum(part):
    part = part + lax.ppermute(part, "tensor", [(0, 1), (1, 0), (2, 3), (3, 2)])
    return part + lax.ppermute(part, "tensor", [(0, 2), (2, 0), (1, 3), (3, 1)])


def gather_rows(shard):
    return lax.all_gather(shard, ROW_AXES, axis=0, tiled=True)


def scatter_rows(grads):
    return lax.psum_scatter(grads, ROW_AXES, scatter_dimension=0, tiled=True).astype(F32)


def fold(values, row_count):
    return jnp.broadcast_to(values, (row_count,)).astype(BF16)[:, None]


def spread_small(values):
    size = lax.axis_size("dp")
    step = 1
    while step < size:
        values = values + lax.ppermute(values, "dp", [(i, i ^ step) for i in range(size)])
        step *= 2
    return values + lax.ppermute(values, "ctx", [(0, 1), (1, 0)])


def body(hidden_in, lengths, w_query, w_keyval, w_output, w_gateup, w_down, gain_attn, gain_mlp, cotangent):
    micro, span, width = hidden_in.shape
    rows = micro * span
    shard_rows = w_query.shape[0]
    q_width = w_query.shape[1]
    ff = w_down.shape[1]
    heads = q_width // HD
    half = HD // 2
    here = lax.axis_index("ctx")
    place = lax.axis_index("tensor")
    choice = ((place == 1) | (place == 2)).astype(jnp.int32).reshape(1)
    sums = Sums(choice)
    join = lambda parts: jnp.concatenate(parts, axis=0)

    gains = jnp.stack([gain_attn, gain_mlp], axis=1)
    gains = jnp.pad(gains, ((0, 0), (0, 126)))
    packed = jnp.concatenate([w_query, w_keyval.reshape(shard_rows, -1), gains], axis=1)
    first = gather_rows(packed)
    qkv_w = first[:, : q_width + 2 * HD]
    gain_pair = first[:, q_width + 2 * HD : q_width + 2 * HD + 2].astype(F32).T
    attn_gain, mlp_gain = gain_pair[0:1], gain_pair[1:2]
    output_w = gather_rows(w_output)
    gateup_w = gather_rows(w_gateup.reshape(shard_rows, 2 * ff))
    down_w = gather_rows(w_down)

    slot_lengths = lax.dynamic_slice_in_dim(lengths, lax.axis_index("dp") * micro, micro)
    slot_of = jnp.repeat(jnp.arange(micro, dtype=jnp.int32), span)
    length_of = jnp.repeat(slot_lengths, span)
    offset = jnp.tile(jnp.arange(span, dtype=jnp.int32), micro)
    position = here * span + offset
    other_position = (1 - here) * span + offset
    live = (position < length_of).astype(F32)[:, None]
    starts = slot_of * SLOT_STEP
    codes = starts + position
    own_codes = jnp.where(position < length_of, codes, NEVER)
    other_codes = jnp.where(other_position < length_of, starts + other_position, NEVER)
    info = jnp.stack([codes, starts])

    frequency = THETA ** (-jnp.arange(0, HD, 2).astype(F32) / HD)
    angles = position.astype(F32)[:, None] * frequency[None, :]
    cosine, sine = jnp.cos(angles), jnp.sin(angles)
    cosine_t, sine_t = cosine.T, sine.T

    hidden_flat = hidden_in.reshape(rows, width)
    seed_flat = cotangent.reshape(rows, width)
    tokens = hidden_flat.astype(F32)

    attn_scale = rms_scale(tokens)
    normed = (tokens * attn_scale * attn_gain).astype(BF16)
    kv_lin = dot(normed, qkv_w[:, q_width:], 1, 0)
    k_low, k_high = kv_lin[:, :half], kv_lin[:, half:HD]
    own_pair = jnp.concatenate(
        [k_low * cosine - k_high * sine, k_high * cosine + k_low * sine, kv_lin[:, HD:]], axis=1
    ).astype(BF16)
    other_pair = lax.ppermute(own_pair, "ctx", [(0, 1), (1, 0)])
    q_lin = dot(qkv_w[:, :q_width], normed, 0, 1).reshape(heads, 2, half, rows) * HD**-0.5
    q_t = jnp.stack(
        [
            q_lin[:, 0] * cosine_t - q_lin[:, 1] * sine_t,
            q_lin[:, 1] * cosine_t + q_lin[:, 0] * sine_t,
        ],
        axis=1,
    ).astype(BF16).reshape(q_width, rows)

    chunk = span // 2
    one, two = slice(0, span), slice(span, 2 * span)
    groups = []
    for at in (one, two):
        pairs = join([own_pair[at], other_pair[at]])
        pairs_t = pairs.T
        key_codes = join([own_codes[at], other_codes[at]])
        groups.append(
            dict(
                flags=block_flags(codes[at], starts[at], key_codes),
                keys=pairs[:, :HD],
                values=pairs[:, HD:],
                keys_t=pairs_t[:HD],
                values_t=pairs_t[HD:],
                codes=key_codes[:, None],
                context=[],
                lse=[],
            )
        )

    def attend_chunk(group, k):
        g = groups[group]
        blocks = 2 * span // BK * chunk // BQ
        lo = group * span + k * chunk
        at = slice(lo, lo + chunk)
        flags = g["flags"][k * blocks : (k + 1) * blocks]
        context, lse = attend(flags, q_t[:, at], info[:, at], g["keys"], g["values_t"], g["codes"])
        g["context"].append(context)
        g["lse"].append(lse)
        return dot(context, output_w, 0, 1)

    def push(k, part):
        for n in range(part.shape[0] // chunk):
            sums.push(k + n, part[n * chunk : (n + 1) * chunk].astype(BF16))

    push(0, attend_chunk(0, 0))
    push(1, attend_chunk(0, 1))
    push(2, attend_chunk(1, 0))
    sums.pair(0, (sums.parts[2],))
    push(3, attend_chunk(1, 1))
    sums.pair(1, (sums.parts[3],))
    sums.total(0)
    sums.pair(2)
    sums.total(1)
    sums.pair(3)
    sums.total(2)

    def middle_of(first, at, after=()):
        return sums.ordered(
            middle_fn, sums.of([first, first + 1]), [(hidden_flat, at.start)], [mlp_gain], [BF16, BF16], after=after, name="middle"
        )

    def forward(normed_rows):
        return dot(normed_rows, gateup_w, 1, 0)

    def products(gateup, seed_rows):
        grad_hidden = dot(seed_rows, down_w, 1, 0)
        gate, up = gateup[:, :ff], gateup[:, ff:]
        sigma = jax.nn.sigmoid(gate)
        activated = gate * sigma
        grad_gate = grad_hidden * up * (sigma * (1.0 + gate * (1.0 - sigma)))
        return (activated * up).astype(BF16), jnp.concatenate([grad_gate, grad_hidden * activated], axis=1).astype(BF16)

    mlp_seed = (seed_flat.astype(F32) * live).astype(BF16)
    attn_out_one, normed_one = middle_of(0, one)
    gateup = forward(normed_one)
    sums.total(3, (gateup,))
    hidden_one, grad_gateup_one = products(gateup, mlp_seed[one])
    push(4, dot(grad_gateup_one, gateup_w, 1, 1))
    attn_out_two, normed_two = middle_of(2, two, (sums.parts[5],))
    gateup = forward(normed_two)
    sums.pair(4, (gateup,))
    hidden_two, grad_gateup_two = products(gateup, mlp_seed[two])
    push(6, held_back(dot(grad_gateup_two, gateup_w, 1, 1), sums.last))
    sums.pair(5, (sums.parts[7],))
    sums.total(4)
    push(8, held_back(dot(hidden_one, down_w, 1, 1), sums.last))
    sums.pair(6, (sums.parts[9],))
    sums.total(5)
    grad_gateup_w = held_back(
        dot(join([normed_one, normed_two]), join([grad_gateup_one, grad_gateup_two]), 0, 0), sums.last
    ).astype(BF16)

    def grad_middle_of(first, at, attn_out, after=()):
        return sums.ordered(
            grad_middle_fn,
            sums.of([first, first + 1]),
            [(hidden_flat, at.start), (attn_out, 0), (seed_flat, at.start), (live, at.start)],
            [mlp_gain],
            [F32, BF16],
            sums=1,
            after=after,
            name="grad_middle",
        )

    def attend_back_group(group, grad_context_t):
        g = groups[group]
        blocks = 2 * span // BK * chunk // BQ
        grad_q, grad_keys, grad_values = [], 0.0, 0.0
        at = slice(group * span, (group + 1) * span)
        got = attend_back(
            g["flags"],
            q_t[:, at],
            grad_context_t,
            jnp.concatenate(g["context"], axis=1),
            jnp.concatenate(g["lse"], axis=1),
            info[:, at],
            cosine_t[:, at],
            sine_t[:, at],
            g["keys"],
            g["values"],
            g["keys_t"],
            g["codes"],
        )
        sent = jnp.concatenate([got[1][span:], got[2][span:]], axis=1)
        returned = lax.ppermute(sent, "ctx", [(0, 1), (1, 0)])
        own_keys = got[1][:span] + returned[:, :HD]
        own_values = got[2][:span] + returned[:, HD:]
        low, high = own_keys[:, :half], own_keys[:, half:]
        cos_rows, sin_rows = cosine[at], sine[at]
        grad_pair = jnp.concatenate([low * cos_rows + high * sin_rows, high * cos_rows - low * sin_rows, own_values], axis=1)
        return got[0], jnp.concatenate([got[0], grad_pair.astype(BF16).T], axis=0)

    grad_middle_one, attn_seed_one, gain_mlp_one = grad_middle_of(4, one, attn_out_one, (grad_gateup_w,))
    sums.pair(7)
    sums.total(6)
    grad_context_t = held_back(dot(output_w, attn_seed_one, 0, 1), sums.last).astype(BF16)
    grad_q_one, grad_qkv_one = attend_back_group(0, grad_context_t)
    sums.pair(8, (grad_q_one,))
    sums.total(7)
    grad_down = held_back(dot(mlp_seed, join([hidden_one, hidden_two]), 0, 0), sums.last).astype(BF16)
    grad_gateup_w = scatter_rows(grad_gateup_w)
    push(12, held_back(dot(grad_qkv_one, qkv_w, 0, 1), grad_down))
    push(10, held_back(dot(hidden_two, down_w, 1, 1), sums.parts[13]))
    grad_middle_two, attn_seed_two, gain_mlp_two = grad_middle_of(6, two, attn_out_two, (sums.parts[11],))
    sums.pair(9)
    sums.total(8)
    grad_context_t = held_back(dot(output_w, attn_seed_two, 0, 1), sums.last).astype(BF16)
    grad_q_two, grad_qkv_two = attend_back_group(1, grad_context_t)
    sums.pair(12, (grad_q_two,))
    sums.total(9)
    push(14, held_back(dot(grad_qkv_two, qkv_w, 0, 1), sums.last))
    grad_down = scatter_rows(grad_down)
    gain_attn_part = 0.0
    for k in range(4):
        at = slice(k * chunk, (k + 1) * chunk)
        gain_attn_part = gain_attn_part + jnp.sum(sums.parts[12 + k].astype(F32) * tokens[at] * attn_scale[at], axis=0)
    sums.pair(13, (sums.parts[15],))
    sums.total(12)
    extra = jnp.concatenate([fold(gain_attn_part, width), fold((gain_mlp_one + gain_mlp_two)[0], width)], axis=1)
    extra = jnp.pad(extra, ((0, 0), (0, 126)))
    grad_qkv_t = jnp.concatenate([grad_qkv_one, grad_qkv_two], axis=1)
    context_t = jnp.concatenate(groups[0]["context"] + groups[1]["context"], axis=1)
    last = jnp.concatenate(
        [
            held_back(dot(normed, grad_qkv_t, 0, 1), sums.last).astype(BF16),
            extra,
            held_back(dot(join([attn_seed_one, attn_seed_two]), context_t, 0, 1), sums.last).astype(BF16),
        ],
        axis=1,
    )

    def result_of(first, at, attn_out, after=()):
        return sums.ordered(
            result_fn,
            sums.of([first, first + 1]),
            [(hidden_flat, at.start), (attn_out, 0), (live, at.start)],
            [],
            [BF16],
            sums=3,
            after=after,
            name="result",
        )

    def input_grad_of(first, at, grad_middle, after=()):
        return sums.ordered(
            input_grad_fn,
            sums.of([first, first + 1]),
            [(hidden_flat, at.start), (grad_middle, 0)],
            [attn_gain],
            [BF16],
            after=after,
            name="input_grad",
        )[0]

    sums.pair(10, (last,))
    sums.total(13)
    last = scatter_rows(last)
    output_one, *squares_one = result_of(8, one, attn_out_one)
    sums.pair(11)
    sums.total(10)
    sums.pair(14, (grad_gateup_w,))
    sums.total(11)
    input_grad_one = input_grad_of(12, one, grad_middle_one)
    sums.pair(15)
    sums.total(14)
    output_two, *squares_two = result_of(10, two, attn_out_two)
    sums.total(15)
    input_grad_two = input_grad_of(14, two, grad_middle_two)
    squares = [jnp.sum(x) + jnp.sum(y) for x, y in zip(squares_one, squares_two)]
    squares = spread_small(jnp.broadcast_to(jnp.stack(squares + [0.0])[None, :], (8, 4)))[0, :3]
    root_means = jnp.sqrt(squares / (jnp.sum(lengths).astype(F32) * width))
    at = q_width + 2 * HD
    return (
        join([output_one, output_two]).reshape(hidden_in.shape),
        join([input_grad_one, input_grad_two]).reshape(hidden_in.shape),
        last[:, :q_width],
        last[:, q_width:at].reshape(w_keyval.shape),
        last[:, at + 128 :],
        grad_gateup_w.reshape(w_gateup.shape),
        grad_down,
        small_sum(last[:, at]),
        last[:, at + 1],
        root_means,
    )


def solution(mesh):
    placed = (
        P("dp", "ctx", None),
        P(),
        P(("dp", "ctx"), "tensor"),
        P(("dp", "ctx"), "tensor", None),
        P(("dp", "ctx"), "tensor"),
        P(("dp", "ctx"), None, "tensor"),
        P(("dp", "ctx"), "tensor"),
        P(("dp", "ctx")),
        P(("dp", "ctx")),
        P("dp", "ctx", None),
    )
    return jax.shard_map(
        body,
        mesh=mesh,
        in_specs=placed,
        out_specs=(
            P("dp", "ctx", None),
            P("dp", "ctx", None),
            P(("dp", "ctx"), "tensor"),
            P(("dp", "ctx"), "tensor", None),
            P(("dp", "ctx"), "tensor"),
            P(("dp", "ctx"), None, "tensor"),
            P(("dp", "ctx"), "tensor"),
            P(("dp", "ctx")),
            P(("dp", "ctx")),
            P(),
        ),
        check_vma=False,
    )
```

```python
import functools

import jax
import jax.numpy as jnp
from jax import lax
from jax.experimental import pallas as pl
from jax.experimental.pallas import tpu as pltpu
from jax.sharding import PartitionSpec as P

HD = 64
EPS = 1e-05
THETA = 10000.0
NEG_FILL = -1e30
SLOT_STEP = 1 << 16
NEVER = 1 << 30
BQ = 256
BK = 256
SIDE = 1
F32 = jnp.float32
BF16 = jnp.bfloat16
SMALL_COST = pl.CostEstimate(flops=1024, bytes_accessed=1024, transcendentals=0)
ROW_AXES = ("dp", "ctx")


def dot(left, right, left_dim, right_dim):
    return lax.dot_general(
        left, right, (((left_dim,), (right_dim,)), ((), ())), preferred_element_type=F32
    )


def rms_scale(values):
    return lax.rsqrt(jnp.mean(values * values, axis=-1, keepdims=True) + EPS)


def mask_bias(key_code, query_info):
    code, start = query_info[0:1, :], query_info[1:2, :]
    allowed = (key_code <= code) & (key_code >= start)
    return jnp.where(allowed, 0.0, NEG_FILL)


def beside(parts):
    return jnp.concatenate(parts, axis=1)


def heads_of(ref, rows):
    return beside([ref[r * HD : (r + 1) * HD, :] for r in rows])


def rows_of(ref, rows):
    return beside([ref[r : r + 1, :] for r in rows])


def attend_kernel(heads, blocks, first, flags, q_ref, info_ref, k_ref, vt_ref, code_ref, o_ref, lse_ref, m_ref, l_ref, acc_ref):
    m_ref[...] = jnp.full_like(m_ref, NEG_FILL)
    l_ref[...] = jnp.zeros_like(l_ref)
    acc_ref[...] = jnp.zeros_like(acc_ref)
    row = first + pl.program_id(0)

    def step(kb, carry):
        @pl.when(flags[row * blocks + kb] > 0)
        def _():
            at = pl.multiple_of(kb * BK, BK)
            keys = k_ref[pl.ds(at, BK), :]
            values_t = vt_ref[:, pl.ds(at, BK)]
            bias = beside([mask_bias(code_ref[pl.ds(at, BK), :], info_ref[...])] * SIDE)
            for h in range(0, heads, SIDE):
                rows = range(h, h + SIDE)
                scores = dot(keys, heads_of(q_ref, rows), 1, 0) + bias
                before = rows_of(m_ref, rows)
                top = jnp.maximum(before, jnp.max(scores, axis=0, keepdims=True))
                shrink = jnp.exp(before - top)
                weights = jnp.exp(scores - top)
                total = shrink * rows_of(l_ref, rows) + jnp.sum(weights, axis=0, keepdims=True)
                out = shrink * heads_of(acc_ref, rows) + dot(values_t, weights.astype(BF16), 1, 0)
                for n, r in enumerate(rows):
                    lanes = slice(n * BQ, (n + 1) * BQ)
                    m_ref[r : r + 1, :] = top[:, lanes]
                    l_ref[r : r + 1, :] = total[:, lanes]
                    acc_ref[r * HD : (r + 1) * HD, :] = out[:, lanes]

        return carry

    lax.fori_loop(0, blocks, step, 0)
    total = l_ref[...]
    total = jnp.where(total == 0.0, 1.0, total)
    lse_ref[...] = m_ref[...] + jnp.log(total)
    for h in range(heads):
        part = slice(h * HD, (h + 1) * HD)
        o_ref[part, :] = (acc_ref[part, :] / total[h : h + 1, :]).astype(BF16)


def attend(flags, q_t, info, keys, values_t, codes, first, base, steps):
    width = q_t.shape[0]
    rows = steps * BQ
    heads = width // HD
    count = keys.shape[0]
    blocks = count // BK
    whole = lambda i, f: (0, 0)
    column = lambda i, f: (0, base + first + i)
    made = lambda i, f: (0, i)
    return pl.pallas_call(
        functools.partial(attend_kernel, heads, blocks, first),
        out_shape=(
            jax.ShapeDtypeStruct((width, rows), BF16),
            jax.ShapeDtypeStruct((heads, rows), F32),
        ),
        grid_spec=pltpu.PrefetchScalarGridSpec(
            num_scalar_prefetch=1,
            grid=(steps,),
            in_specs=[
                pl.BlockSpec((width, BQ), column),
                pl.BlockSpec((2, BQ), column),
                pl.BlockSpec((count, HD), whole),
                pl.BlockSpec((HD, count), whole),
                pl.BlockSpec((count, 1), whole),
            ],
            out_specs=[pl.BlockSpec((width, BQ), made), pl.BlockSpec((heads, BQ), made)],
            scratch_shapes=[
                pltpu.VMEM((heads, BQ), F32),
                pltpu.VMEM((heads, BQ), F32),
                pltpu.VMEM((width, BQ), F32),
            ],
        ),
        compiler_params=pltpu.CompilerParams(vmem_limit_bytes=24 << 20),
        cost_estimate=SMALL_COST,
        name="attend",
    )(flags, q_t, info, keys, values_t, codes)


def attend_back_kernel(
    heads, blocks, first, carried, flags, q_ref, do_ref, o_ref, lse_ref, info_ref, cos_ref, sin_ref, k_ref, v_ref, kt_ref,
    code_ref, *refs
):
    row = first
    dq_ref, own_ref, other_ref, acc_ref, delta_ref, dk_ref, dv_ref = refs[-7:]
    dk_ref[...] = jnp.zeros_like(dk_ref)
    dv_ref[...] = jnp.zeros_like(dv_ref)

    acc_ref[...] = jnp.zeros_like(acc_ref)
    for h in range(heads):
        part = slice(h * HD, (h + 1) * HD)
        delta_ref[h : h + 1, :] = jnp.sum(
            do_ref[part, :].astype(F32) * o_ref[part, :].astype(F32), axis=0, keepdims=True
        )

    def step(kb, carry):
        @pl.when(flags[row * blocks + kb] > 0)
        def _():
            at = pl.multiple_of(kb * BK, BK)
            keys = k_ref[pl.ds(at, BK), :]
            values = v_ref[pl.ds(at, BK), :]
            keys_t = kt_ref[:, pl.ds(at, BK)]
            bias = beside([mask_bias(code_ref[pl.ds(at, BK), :], info_ref[...])] * SIDE)
            grad_keys = jnp.zeros((BK, HD), F32)
            grad_values = jnp.zeros((BK, HD), F32)
            for h in range(0, heads, SIDE):
                rows = range(h, h + SIDE)
                queries = heads_of(q_ref, rows)
                grads = heads_of(do_ref, rows)
                weights = jnp.exp(dot(keys, queries, 1, 0) + bias - rows_of(lse_ref, rows))
                grad_weights = dot(values, grads, 1, 0)
                raw = (weights * (grad_weights - rows_of(delta_ref, rows))).astype(BF16)
                grad_values = grad_values + dot(weights.astype(BF16), grads, 1, 1)
                grad_keys = grad_keys + dot(raw, queries, 1, 1)
                out = dot(keys_t, raw, 1, 0)
                for n, r in enumerate(rows):
                    acc_ref[r * HD : (r + 1) * HD, :] += out[:, n * BQ : (n + 1) * BQ]
            dk_ref[pl.ds(at, BK), :] += grad_keys
            dv_ref[pl.ds(at, BK), :] += grad_values

        return carry

    lax.fori_loop(0, blocks, step, 0)
    cosine, sine = cos_ref[...], sin_ref[...]
    half = HD // 2
    for h in range(heads):
        lower = acc_ref[h * HD : h * HD + half, :] * HD**-0.5
        upper = acc_ref[h * HD + half : (h + 1) * HD, :] * HD**-0.5
        dq_ref[h * HD : h * HD + half, :] = (lower * cosine + upper * sine).astype(BF16)
        dq_ref[h * HD + half : (h + 1) * HD, :] = (upper * cosine - lower * sine).astype(BF16)
    half_count = own_ref.shape[0]
    for ref, lo, more in ((own_ref, 0, refs[0]), (other_ref, half_count, refs[1])):
        made = beside([dk_ref[lo : lo + half_count, :], dv_ref[lo : lo + half_count, :]])
        ref[...] = made + more[...] if carried else made


def attend_back(flags, q_t, grad_t, o_t, lse, info, cosine_t, sine_t, keys, values, keys_t, codes, first, base, carry):
    width = q_t.shape[0]
    heads = width // HD
    count = keys.shape[0]
    blocks = count // BK
    whole = lambda i, f: (0, 0)
    column = lambda i, f: (0, base + first)
    pair = pl.BlockSpec((count // 2, 2 * HD), whole)
    return pl.pallas_call(
        functools.partial(attend_back_kernel, heads, blocks, first, carry is not None),
        out_shape=(
            jax.ShapeDtypeStruct((width, BQ), BF16),
            jax.ShapeDtypeStruct((count // 2, 2 * HD), F32),
            jax.ShapeDtypeStruct((count // 2, 2 * HD), F32),
        ),
        grid_spec=pltpu.PrefetchScalarGridSpec(
            num_scalar_prefetch=1,
            grid=(1,),
            in_specs=[
                pl.BlockSpec((width, BQ), column),
                pl.BlockSpec((width, BQ), lambda i, f: (0, first)),
                pl.BlockSpec((width, BQ), whole),
                pl.BlockSpec((heads, BQ), whole),
                pl.BlockSpec((2, BQ), column),
                pl.BlockSpec((HD // 2, BQ), column),
                pl.BlockSpec((HD // 2, BQ), column),
                pl.BlockSpec((count, HD), whole),
                pl.BlockSpec((count, HD), whole),
                pl.BlockSpec((HD, count), whole),
                pl.BlockSpec((count, 1), whole),
            ]
            + ([pair, pair] if carry is not None else []),
            out_specs=[pl.BlockSpec((width, BQ), whole), pair, pair],
            scratch_shapes=[
                pltpu.VMEM((width, BQ), F32),
                pltpu.VMEM((heads, BQ), F32),
                pltpu.VMEM((count, HD), F32),
                pltpu.VMEM((count, HD), F32),
            ],
        ),
        compiler_params=pltpu.CompilerParams(vmem_limit_bytes=32 << 20),
        cost_estimate=SMALL_COST,
        name="attend_back",
    )(flags, q_t, grad_t, o_t, lse, info, cosine_t, sine_t, keys, values, keys_t, codes, *(carry or ()))


def block_flags(codes, starts, key_codes):
    top = jnp.max(codes.reshape(-1, BQ), axis=1)
    low = jnp.min(starts.reshape(-1, BQ), axis=1)
    blocks = key_codes.reshape(-1, BK)
    key_low = jnp.min(blocks, axis=1)
    key_top = jnp.max(jnp.where(blocks < NEVER, blocks, -1), axis=1)
    seen = (key_low[None, :] <= top[:, None]) & (key_top[None, :] >= low[:, None])
    return seen.astype(jnp.int32).reshape(-1)


def rowwise_kernel(fn, bounds, lists, flats, consts, outs, choice, *refs):
    pieces = len(bounds)
    n_list = lists * pieces
    step = pl.program_id(0)
    flat_refs = refs[n_list : n_list + flats]
    const_refs = refs[n_list + flats : n_list + flats + consts]
    out_refs = refs[len(refs) - outs[0] - outs[1] : len(refs) - outs[1]]
    sum_refs = refs[len(refs) - outs[1] :]

    if outs[1]:
        @pl.when(step == 0)
        def _():
            for ref in sum_refs:
                ref[...] = jnp.zeros_like(ref)

    for j, (lo, hi) in enumerate(bounds):
        @pl.when((step >= lo) & (step < hi))
        def _():
            got, sums = fn(
                choice[0],
                [refs[k * pieces + j][...].astype(F32) for k in range(lists)],
                [ref[...].astype(F32) for ref in flat_refs],
                [ref[...] for ref in const_refs],
            )
            for ref, value in zip(out_refs, got):
                ref[...] = value.astype(ref.dtype)
            for ref, value in zip(sum_refs, sums):
                ref[...] += value


def tile_of(size):
    return next(tile for tile in (128, 160, 96, 64, 32, 16) if size % tile == 0)


def rowwise(fn, choice, lists, flats, consts, outs, sums=0, after=(), name="rowwise"):
    tile = tile_of(lists[0][0].shape[0])
    sizes = [piece.shape[0] // tile for piece in lists[0]]
    width = lists[0][0].shape[1]
    bounds, lo = [], 0
    for size in sizes:
        bounds.append((lo, lo + size))
        lo += size
    total = lo

    def piece_map(lo, size):
        return lambda i, c: (jnp.clip(i - lo, 0, size - 1), 0)

    in_specs, operands = [], []
    for pieces in lists:
        for piece, (lo, hi) in zip(pieces, bounds):
            in_specs.append(pl.BlockSpec((tile, width), piece_map(lo, hi - lo)))
            operands.append(piece)
    for array, first in flats:
        offset = first // tile
        in_specs.append(pl.BlockSpec((tile, array.shape[1]), lambda i, c, offset=offset: (i + offset, 0)))
        operands.append(array)
    for array in consts:
        in_specs.append(pl.BlockSpec((1, array.shape[1]), lambda i, c: (0, 0)))
        operands.append(array)
    for array in after:
        in_specs.append(pl.BlockSpec(memory_space=pl.ANY))
        operands.append(array)
    rows = total * tile
    return pl.pallas_call(
        functools.partial(rowwise_kernel, fn, bounds, len(lists), len(flats), len(consts), (len(outs), sums)),
        out_shape=[jax.ShapeDtypeStruct((rows, width), dtype) for dtype in outs]
        + [jax.ShapeDtypeStruct((1, width), F32)] * sums,
        grid_spec=pltpu.PrefetchScalarGridSpec(
            num_scalar_prefetch=1,
            grid=(total,),
            in_specs=in_specs,
            out_specs=[pl.BlockSpec((tile, width), lambda i, c: (i, 0))] * len(outs)
            + [pl.BlockSpec((1, width), lambda i, c: (0, 0))] * sums,
        ),
        compiler_params=pltpu.CompilerParams(vmem_limit_bytes=32 << 20),
        cost_estimate=SMALL_COST,
        name=name,
    )(choice, *operands)


def add_fn(choice, lists, flats, consts):
    return [lists[0] + lists[1]], []


def pick(choice, total, third):
    return jnp.where(choice > 0, total, third)


def row_scale(values):
    return lax.rsqrt(jnp.mean(values * values, axis=1, keepdims=True) + EPS)


def middle_fn(choice, lists, flats, consts):
    branch = pick(choice, lists[0], lists[1])
    middle = flats[0] + branch
    return [branch, middle * row_scale(middle) * consts[0]], []


def column_sum(values):
    return jnp.sum(values, axis=0, keepdims=True)


def grad_middle_fn(choice, lists, flats, consts):
    grad = pick(choice, lists[0], lists[1])
    tokens, branch, seed, live = flats
    middle = tokens + branch
    scale = row_scale(middle)
    weighted = grad * consts[0]
    mean = jnp.mean(weighted * middle, axis=1, keepdims=True)
    out = seed * live + scale * weighted - middle * scale**3 * mean
    return [out, out], [column_sum(grad * middle * scale)]


def input_grad_fn(choice, lists, flats, consts):
    grad = pick(choice, lists[0], lists[1])
    tokens, grad_middle = flats
    scale = row_scale(tokens)
    weighted = grad * consts[0]
    mean = jnp.mean(weighted * tokens, axis=1, keepdims=True)
    return [grad_middle + scale * weighted - tokens * scale**3 * mean], []


def gain_fn(choice, lists, flats, consts):
    return [], [column_sum(lists[0] * flats[0] * row_scale(flats[0]))]


def result_fn(choice, lists, flats, consts):
    mlp_branch = pick(choice, lists[0], lists[1])
    tokens, branch, live = flats
    result = (tokens + branch + mlp_branch) * live
    return [result], [
        column_sum(result * result),
        column_sum(branch * branch * live),
        column_sum(mlp_branch * mlp_branch * live),
    ]


def pair_back_kernel(own_ref, returned_ref, cos_ref, sin_ref, out_ref):
    both = (own_ref[...] + returned_ref[...]).T
    half = HD // 2
    low, high = both[:half, :], both[half:HD, :]
    cosine, sine = cos_ref[...], sin_ref[...]
    out_ref[:half, :] = (low * cosine + high * sine).astype(BF16)
    out_ref[half:HD, :] = (high * cosine - low * sine).astype(BF16)
    out_ref[HD:, :] = both[HD:, :].astype(BF16)


def pair_back(own, returned, cosine_t, sine_t, block):
    rows = own.shape[0]
    whole = pl.BlockSpec((rows, 2 * HD), lambda i: (0, 0))
    table = pl.BlockSpec((HD // 2, rows), lambda i: (0, block))
    return pl.pallas_call(
        pair_back_kernel,
        out_shape=jax.ShapeDtypeStruct((2 * HD, rows), BF16),
        grid_spec=pltpu.PrefetchScalarGridSpec(
            num_scalar_prefetch=0,
            grid=(1,),
            in_specs=[whole, whole, table, table],
            out_specs=pl.BlockSpec((2 * HD, rows), lambda i: (0, 0)),
        ),
        cost_estimate=SMALL_COST,
        name="pair_back",
    )(own, returned, cosine_t, sine_t)


def send_in(part):
    return lax.ppermute(part, "tensor", [(0, 1), (3, 2)])


def send_across(pair):
    return lax.ppermute(pair, "tensor", [(1, 2), (2, 1)])


def send_out(total):
    return lax.ppermute(total, "tensor", [(1, 0), (2, 3)])


def held_back(value, dep):
    return value + dep[:1, :1].astype(F32) * 0.0


class Sums:
    def __init__(self, choice):
        self.choice = choice
        self.last = None
        self.order = []
        self.parts, self.firsts, self.pairs, self.seconds, self.totals, self.thirds = {}, {}, {}, {}, {}, {}

    def ordered(self, fn, *args, **more):
        after = tuple(more.pop("after", ()))
        if self.last is not None:
            after += (self.last,)
        got = rowwise(fn, self.choice, *args, after=after, **more)
        self.last = got[0]
        return got

    def ordered_sum(self, fn, lists, flats, name):
        got = rowwise(fn, self.choice, lists, flats, [], [], sums=1, after=(self.last,), name=name)
        self.last = got[0]
        return got[0]

    def push(self, k, part):
        self.order.append(k)
        self.parts[k] = part
        self.firsts[k] = send_in(part)

    def pair(self, k, after=()):
        spot = self.order.index(k)
        if spot == 3:
            after = tuple(after) + (self.thirds[self.order[0]],)
        both = [[self.parts[k]], [self.firsts[k]]]
        self.pairs[k] = self.ordered(add_fn, both, [], [], [BF16], after=after, name="pair")[0]
        self.seconds[k] = send_across(self.pairs[k])

    def total(self, k, after=()):
        both = [[self.pairs[k]], [self.seconds[k]]]
        self.totals[k] = self.ordered(add_fn, both, [], [], [BF16], after=after, name="total")[0]
        self.thirds[k] = send_out(self.totals[k])

    def of(self, picked):
        return [self.totals[k] for k in picked], [self.thirds[k] for k in picked]


def small_sum(part):
    part = part + lax.ppermute(part, "tensor", [(0, 1), (1, 0), (2, 3), (3, 2)])
    return part + lax.ppermute(part, "tensor", [(0, 2), (2, 0), (1, 3), (3, 1)])


def gather_rows(shard):
    return lax.all_gather(shard, ROW_AXES, axis=0, tiled=True)


def same(ref, *rest):
    pass


def once(value, after):
    anywhere = pl.BlockSpec(memory_space=pl.ANY)
    return pl.pallas_call(
        same,
        out_shape=jax.ShapeDtypeStruct(value.shape, value.dtype),
        in_specs=[anywhere] * (1 + len(after)),
        out_specs=anywhere,
        input_output_aliases={0: 0},
        cost_estimate=SMALL_COST,
        name="once",
    )(value, *after)


def scatter_rows(grads):
    return lax.psum_scatter(grads, ROW_AXES, scatter_dimension=0, tiled=True).astype(F32)


def fold(values, row_count):
    return jnp.broadcast_to(values, (row_count,)).astype(BF16)[:, None]


def spread_small(values):
    size = lax.axis_size("dp")
    step = 1
    while step < size:
        values = values + lax.ppermute(values, "dp", [(i, i ^ step) for i in range(size)])
        step *= 2
    return values + lax.ppermute(values, "ctx", [(0, 1), (1, 0)])


def body(hidden_in, lengths, w_query, w_keyval, w_output, w_gateup, w_down, gain_attn, gain_mlp, cotangent):
    micro, span, width = hidden_in.shape
    rows = micro * span
    shard_rows = w_query.shape[0]
    q_width = w_query.shape[1]
    ff = w_down.shape[1]
    heads = q_width // HD
    half = HD // 2
    here = lax.axis_index("ctx")
    place = lax.axis_index("tensor")
    choice = ((place == 1) | (place == 2)).astype(jnp.int32).reshape(1)
    sums = Sums(choice)
    join = lambda parts: jnp.concatenate(parts, axis=0)

    gains = jnp.stack([gain_attn, gain_mlp], axis=1)
    gains = jnp.pad(gains, ((0, 0), (0, 126)))
    packed = jnp.concatenate([w_query, w_keyval.reshape(shard_rows, -1), gains], axis=1)
    first = gather_rows(packed)
    qkv_w = first[:, : q_width + 2 * HD]
    gain_pair = first[:, q_width + 2 * HD : q_width + 2 * HD + 2].astype(F32).T
    attn_gain, mlp_gain = gain_pair[0:1], gain_pair[1:2]
    output_w = gather_rows(w_output)
    gateup_w = gather_rows(w_gateup.reshape(shard_rows, 2 * ff))
    down_w = gather_rows(w_down)

    slot_lengths = lax.dynamic_slice_in_dim(lengths, lax.axis_index("dp") * micro, micro)
    slot_of = jnp.repeat(jnp.arange(micro, dtype=jnp.int32), span)
    length_of = jnp.repeat(slot_lengths, span)
    offset = jnp.tile(jnp.arange(span, dtype=jnp.int32), micro)
    position = here * span + offset
    other_position = (1 - here) * span + offset
    live = (position < length_of).astype(F32)[:, None]
    starts = slot_of * SLOT_STEP
    codes = starts + position
    own_codes = jnp.where(position < length_of, codes, NEVER)
    other_codes = jnp.where(other_position < length_of, starts + other_position, NEVER)
    info = jnp.stack([codes, starts])

    frequency = THETA ** (-jnp.arange(0, HD, 2).astype(F32) / HD)
    angles = position.astype(F32)[:, None] * frequency[None, :]
    cosine, sine = jnp.cos(angles), jnp.sin(angles)
    cosine_t, sine_t = cosine.T, sine.T

    hidden_flat = hidden_in.reshape(rows, width)
    seed_flat = cotangent.reshape(rows, width)
    tokens = hidden_flat.astype(F32)

    attn_scale = rms_scale(tokens)
    normed = (tokens * attn_scale * attn_gain).astype(BF16)
    kv_lin = dot(normed, qkv_w[:, q_width:], 1, 0)
    k_low, k_high = kv_lin[:, :half], kv_lin[:, half:HD]
    own_pair = jnp.concatenate(
        [k_low * cosine - k_high * sine, k_high * cosine + k_low * sine, kv_lin[:, HD:]], axis=1
    ).astype(BF16)
    other_pair = lax.ppermute(own_pair, "ctx", [(0, 1), (1, 0)])
    q_lin = dot(qkv_w[:, :q_width], normed, 0, 1).reshape(heads, 2, half, rows) * HD**-0.5
    q_t = jnp.stack(
        [
            q_lin[:, 0] * cosine_t - q_lin[:, 1] * sine_t,
            q_lin[:, 1] * cosine_t + q_lin[:, 0] * sine_t,
        ],
        axis=1,
    ).astype(BF16).reshape(q_width, rows)

    chunk = span // 2
    one, two = slice(0, span), slice(span, 2 * span)
    groups = []
    for at in (one, two):
        pairs = join([own_pair[at], other_pair[at]])
        pairs_t = pairs.T
        key_codes = join([own_codes[at], other_codes[at]])
        groups.append(
            dict(
                flags=block_flags(codes[at], starts[at], key_codes),
                keys=pairs[:, :HD],
                values=pairs[:, HD:],
                keys_t=pairs_t[:HD],
                values_t=pairs_t[HD:],
                codes=key_codes[:, None],
                context=[],
                lse=[],
            )
        )

    def attend_chunk(group, k):
        g = groups[group]
        context, lse = attend(
            g["flags"], q_t, info, g["keys"], g["values_t"], g["codes"], k, group * span // BQ, chunk // BQ
        )
        g["context"].append(context)
        g["lse"].append(lse)
        return dot(context, output_w, 0, 1)

    def push(k, part, size=chunk):
        for n in range(part.shape[0] // size):
            sums.push(k + n, part[n * size : (n + 1) * size].astype(BF16))

    push(0, attend_chunk(0, 0))
    push(1, attend_chunk(0, 1))
    push(2, attend_chunk(1, 0))
    sums.pair(0, (sums.parts[2],))
    push(3, attend_chunk(1, 1))
    sums.pair(1, (sums.parts[3],))
    sums.total(0)
    sums.pair(2)
    sums.total(1)
    sums.pair(3)
    sums.total(2)

    def middle_of(first, at, after=()):
        return sums.ordered(
            middle_fn, sums.of([first, first + 1]), [(hidden_flat, at.start)], [mlp_gain], [BF16, BF16], after=after, name="middle"
        )

    def forward(normed_rows):
        return dot(normed_rows, gateup_w, 1, 0)

    def products(gateup, seed_rows):
        grad_hidden = dot(seed_rows, down_w, 1, 0)
        gate, up = gateup[:, :ff], gateup[:, ff:]
        sigma = jax.nn.sigmoid(gate)
        activated = gate * sigma
        grad_gate = grad_hidden * up * (sigma * (1.0 + gate * (1.0 - sigma)))
        return (activated * up).astype(BF16), jnp.concatenate([grad_gate, grad_hidden * activated], axis=1).astype(BF16)

    mlp_seed = (seed_flat.astype(F32) * live).astype(BF16)
    attn_out_one, normed_one = middle_of(0, one)
    gateup = forward(normed_one)
    sums.total(3, (gateup,))
    hidden_one, grad_gateup_one = products(gateup, mlp_seed[one])
    push(4, dot(grad_gateup_one, gateup_w, 1, 1))
    attn_out_two, normed_two = middle_of(2, two, (sums.parts[5],))
    gateup = forward(normed_two)
    sums.pair(4, (gateup,))
    hidden_two, grad_gateup_two = products(gateup, mlp_seed[two])
    push(6, held_back(dot(grad_gateup_two, gateup_w, 1, 1), sums.last))
    sums.pair(5, (sums.parts[7],))
    sums.total(4)
    hidden = join([hidden_one, hidden_two])
    push(8, held_back(dot(hidden_one, down_w, 1, 1), sums.last), span)
    push(10, held_back(dot(hidden_two, down_w, 1, 1), sums.parts[8]), span)
    sums.pair(6, (sums.parts[10], sums.thirds[4]))
    sums.total(5)
    grad_gateup_w = held_back(
        dot(join([normed_one, normed_two]), join([grad_gateup_one, grad_gateup_two]), 0, 0), sums.last
    ).astype(BF16)
    sums.pair(7, (grad_gateup_w, sums.thirds[5]))
    sums.total(6)
    grad_gateup_w = scatter_rows(once(grad_gateup_w, (sums.totals[6],)))

    def grad_middle_of(first, at, attn_out, after=()):
        return sums.ordered(
            grad_middle_fn,
            sums.of([first, first + 1]),
            [(hidden_flat, at.start), (attn_out, 0), (seed_flat, at.start), (live, at.start)],
            [mlp_gain],
            [F32, BF16],
            sums=1,
            after=after,
            name="grad_middle",
        )

    def attend_back_group(group, seeds):
        g = groups[group]
        grad_context_t = held_back(dot(output_w, seeds, 0, 1), sums.last).astype(BF16)
        carry, grads = None, []
        for k in range(2):
            grad_q, *carry = attend_back(
                g["flags"], q_t, grad_context_t, g["context"][k], g["lse"][k], info, cosine_t, sine_t,
                g["keys"], g["values"], g["keys_t"], g["codes"], k, group * span // BQ, carry,
            )
            grads.append(grad_q)
        returned = lax.ppermute(carry[1], "ctx", [(0, 1), (1, 0)])
        grad_pair = pair_back(carry[0], returned, cosine_t, sine_t, group)
        g["grad"] = jnp.concatenate([jnp.concatenate(grads, axis=1), grad_pair], axis=0)
        return grads[1]

    def attn_back_of(group):
        return dot(groups[group]["grad"], qkv_w, 0, 1)

    grad_middle_one, attn_seed_one, gain_mlp_one = grad_middle_of(4, one, attn_out_one)
    sums.total(7, (sums.thirds[6],))
    done = attend_back_group(0, attn_seed_one)
    sums.pair(8, (done,))
    grad_middle_two, attn_seed_two, gain_mlp_two = grad_middle_of(6, two, attn_out_two)
    push(12, held_back(attn_back_of(0), sums.last))
    done = attend_back_group(1, attn_seed_two)
    sums.pair(10, (done, sums.parts[13]))
    sums.total(8)
    grad_down = held_back(dot(mlp_seed, hidden, 0, 0), sums.last).astype(BF16)
    push(14, held_back(attn_back_of(1), grad_down))
    sums.pair(12, (sums.parts[15],))
    sums.pair(13, (sums.thirds[8],))
    sums.total(10)
    grad_down = scatter_rows(once(grad_down, (sums.totals[10], grad_gateup_w)))
    sums.total(12)
    gain_attn_part = sums.ordered_sum(
        gain_fn, [[sums.parts[12 + k] for k in range(4)]], [(hidden_flat, 0)], "gain_attn"
    )
    extra = jnp.concatenate([fold(gain_attn_part[0], width), fold((gain_mlp_one + gain_mlp_two)[0], width)], axis=1)
    extra = jnp.pad(extra, ((0, 0), (0, 126)))
    grad_qkv_t = jnp.concatenate([groups[0]["grad"], groups[1]["grad"]], axis=1)
    context_t = jnp.concatenate(groups[0]["context"] + groups[1]["context"], axis=1)
    last = jnp.concatenate(
        [
            held_back(dot(normed, grad_qkv_t, 0, 1), sums.last).astype(BF16),
            extra,
            held_back(dot(join([attn_seed_one, attn_seed_two]), context_t, 0, 1), sums.last).astype(BF16),
        ],
        axis=1,
    )

    def result_of(first, at, attn_out, after=()):
        return sums.ordered(
            result_fn,
            sums.of([first]),
            [(hidden_flat, at.start), (attn_out, 0), (live, at.start)],
            [],
            [BF16],
            sums=3,
            after=after,
            name="result",
        )

    def input_grad_of(first, at, grad_middle, after=()):
        return sums.ordered(
            input_grad_fn,
            sums.of([first, first + 1]),
            [(hidden_flat, at.start), (grad_middle, 0)],
            [attn_gain],
            [BF16],
            after=after,
            name="input_grad",
        )[0]

    sums.pair(14, (last,))
    sums.total(13)
    sums.pair(15, (sums.thirds[10],))
    sums.total(14)
    last = scatter_rows(once(last, (sums.totals[14], grad_down)))
    sums.total(15)
    output_one, *squares_one = result_of(8, one, attn_out_one)
    output_two, *squares_two = result_of(10, two, attn_out_two)
    input_grad_one = input_grad_of(12, one, grad_middle_one)
    input_grad_two = input_grad_of(14, two, grad_middle_two)
    squares = [jnp.sum(x) + jnp.sum(y) for x, y in zip(squares_one, squares_two)]
    squares = spread_small(jnp.broadcast_to(jnp.stack(squares + [0.0])[None, :], (8, 4)))[0, :3]
    root_means = jnp.sqrt(squares / (jnp.sum(lengths).astype(F32) * width))
    at = q_width + 2 * HD
    return (
        join([output_one, output_two]).reshape(hidden_in.shape),
        join([input_grad_one, input_grad_two]).reshape(hidden_in.shape),
        last[:, :q_width],
        last[:, q_width:at].reshape(w_keyval.shape),
        last[:, at + 128 :],
        grad_gateup_w.reshape(w_gateup.shape),
        grad_down,
        small_sum(last[:, at]),
        last[:, at + 1],
        root_means,
    )


def solution(mesh):
    placed = (
        P("dp", "ctx", None),
        P(),
        P(("dp", "ctx"), "tensor"),
        P(("dp", "ctx"), "tensor", None),
        P(("dp", "ctx"), "tensor"),
        P(("dp", "ctx"), None, "tensor"),
        P(("dp", "ctx"), "tensor"),
        P(("dp", "ctx")),
        P(("dp", "ctx")),
        P("dp", "ctx", None),
    )
    return jax.shard_map(
        body,
        mesh=mesh,
        in_specs=placed,
        out_specs=(
            P("dp", "ctx", None),
            P("dp", "ctx", None),
            P(("dp", "ctx"), "tensor"),
            P(("dp", "ctx"), "tensor", None),
            P(("dp", "ctx"), "tensor"),
            P(("dp", "ctx"), None, "tensor"),
            P(("dp", "ctx"), "tensor"),
            P(("dp", "ctx")),
            P(("dp", "ctx")),
            P(),
        ),
        check_vma=False,
    )
```

```python
import functools

import jax
import jax.numpy as jnp
from jax import lax
from jax.experimental import pallas as pl
from jax.experimental.pallas import tpu as pltpu
from jax.sharding import PartitionSpec as P

HD = 64
EPS = 1e-05
THETA = 10000.0
NEG_FILL = -1e30
SLOT_STEP = 1 << 16
NEVER = 1 << 30
BQ = 256
BK = 256
SIDE = 1
F32 = jnp.float32
BF16 = jnp.bfloat16
SMALL_COST = pl.CostEstimate(flops=1024, bytes_accessed=1024, transcendentals=0)
ROW_AXES = ("dp", "ctx")


def dot(left, right, left_dim, right_dim):
    return lax.dot_general(
        left, right, (((left_dim,), (right_dim,)), ((), ())), preferred_element_type=F32
    )


def rms_scale(values):
    return lax.rsqrt(jnp.mean(values * values, axis=-1, keepdims=True) + EPS)


def mask_bias(key_code, query_info):
    code, start = query_info[0:1, :], query_info[1:2, :]
    allowed = (key_code <= code) & (key_code >= start)
    return jnp.where(allowed, 0.0, NEG_FILL)


def beside(parts):
    return jnp.concatenate(parts, axis=1)


def heads_of(ref, rows):
    return beside([ref[r * HD : (r + 1) * HD, :] for r in rows])


def rows_of(ref, rows):
    return beside([ref[r : r + 1, :] for r in rows])


def attend_kernel(heads, blocks, first, flags, q_ref, info_ref, k_ref, vt_ref, code_ref, o_ref, lse_ref, m_ref, l_ref, acc_ref):
    m_ref[...] = jnp.full_like(m_ref, NEG_FILL)
    l_ref[...] = jnp.zeros_like(l_ref)
    acc_ref[...] = jnp.zeros_like(acc_ref)
    row = first + pl.program_id(0)

    def step(kb, carry):
        @pl.when(flags[row * blocks + kb] > 0)
        def _():
            at = pl.multiple_of(kb * BK, BK)
            keys = k_ref[pl.ds(at, BK), :]
            values_t = vt_ref[:, pl.ds(at, BK)]
            bias = beside([mask_bias(code_ref[pl.ds(at, BK), :], info_ref[...])] * SIDE)
            for h in range(0, heads, SIDE):
                rows = range(h, h + SIDE)
                scores = dot(keys, heads_of(q_ref, rows), 1, 0) + bias
                before = rows_of(m_ref, rows)
                top = jnp.maximum(before, jnp.max(scores, axis=0, keepdims=True))
                shrink = jnp.exp(before - top)
                weights = jnp.exp(scores - top)
                total = shrink * rows_of(l_ref, rows) + jnp.sum(weights, axis=0, keepdims=True)
                out = shrink * heads_of(acc_ref, rows) + dot(values_t, weights.astype(BF16), 1, 0)
                for n, r in enumerate(rows):
                    lanes = slice(n * BQ, (n + 1) * BQ)
                    m_ref[r : r + 1, :] = top[:, lanes]
                    l_ref[r : r + 1, :] = total[:, lanes]
                    acc_ref[r * HD : (r + 1) * HD, :] = out[:, lanes]

        return carry

    lax.fori_loop(0, blocks, step, 0)
    total = l_ref[...]
    total = jnp.where(total == 0.0, 1.0, total)
    lse_ref[...] = m_ref[...] + jnp.log(total)
    for h in range(heads):
        part = slice(h * HD, (h + 1) * HD)
        o_ref[part, :] = (acc_ref[part, :] / total[h : h + 1, :]).astype(BF16)


def attend(flags, q_t, info, keys, values_t, codes, first, base, steps):
    width = q_t.shape[0]
    rows = steps * BQ
    heads = width // HD
    count = keys.shape[0]
    blocks = count // BK
    whole = lambda i, f: (0, 0)
    column = lambda i, f: (0, base + first + i)
    made = lambda i, f: (0, i)
    return pl.pallas_call(
        functools.partial(attend_kernel, heads, blocks, first),
        out_shape=(
            jax.ShapeDtypeStruct((width, rows), BF16),
            jax.ShapeDtypeStruct((heads, rows), F32),
        ),
        grid_spec=pltpu.PrefetchScalarGridSpec(
            num_scalar_prefetch=1,
            grid=(steps,),
            in_specs=[
                pl.BlockSpec((width, BQ), column),
                pl.BlockSpec((2, BQ), column),
                pl.BlockSpec((count, HD), whole),
                pl.BlockSpec((HD, count), whole),
                pl.BlockSpec((count, 1), whole),
            ],
            out_specs=[pl.BlockSpec((width, BQ), made), pl.BlockSpec((heads, BQ), made)],
            scratch_shapes=[
                pltpu.VMEM((heads, BQ), F32),
                pltpu.VMEM((heads, BQ), F32),
                pltpu.VMEM((width, BQ), F32),
            ],
        ),
        compiler_params=pltpu.CompilerParams(vmem_limit_bytes=24 << 20),
        cost_estimate=SMALL_COST,
        name="attend",
    )(flags, q_t, info, keys, values_t, codes)


def attend_back_kernel(
    heads, blocks, first, carried, flags, q_ref, do_ref, o_ref, lse_ref, info_ref, cos_ref, sin_ref, k_ref, v_ref, kt_ref,
    code_ref, *refs
):
    row = first
    dq_ref, own_ref, other_ref, acc_ref, delta_ref, dk_ref, dv_ref = refs[-7:]
    dk_ref[...] = jnp.zeros_like(dk_ref)
    dv_ref[...] = jnp.zeros_like(dv_ref)

    acc_ref[...] = jnp.zeros_like(acc_ref)
    for h in range(heads):
        part = slice(h * HD, (h + 1) * HD)
        delta_ref[h : h + 1, :] = jnp.sum(
            do_ref[part, :].astype(F32) * o_ref[part, :].astype(F32), axis=0, keepdims=True
        )

    def step(kb, carry):
        @pl.when(flags[row * blocks + kb] > 0)
        def _():
            at = pl.multiple_of(kb * BK, BK)
            keys = k_ref[pl.ds(at, BK), :]
            values = v_ref[pl.ds(at, BK), :]
            keys_t = kt_ref[:, pl.ds(at, BK)]
            bias = beside([mask_bias(code_ref[pl.ds(at, BK), :], info_ref[...])] * SIDE)
            grad_keys = jnp.zeros((BK, HD), F32)
            grad_values = jnp.zeros((BK, HD), F32)
            for h in range(0, heads, SIDE):
                rows = range(h, h + SIDE)
                queries = heads_of(q_ref, rows)
                grads = heads_of(do_ref, rows)
                weights = jnp.exp(dot(keys, queries, 1, 0) + bias - rows_of(lse_ref, rows))
                grad_weights = dot(values, grads, 1, 0)
                raw = (weights * (grad_weights - rows_of(delta_ref, rows))).astype(BF16)
                grad_values = grad_values + dot(weights.astype(BF16), grads, 1, 1)
                grad_keys = grad_keys + dot(raw, queries, 1, 1)
                out = dot(keys_t, raw, 1, 0)
                for n, r in enumerate(rows):
                    acc_ref[r * HD : (r + 1) * HD, :] += out[:, n * BQ : (n + 1) * BQ]
            dk_ref[pl.ds(at, BK), :] += grad_keys
            dv_ref[pl.ds(at, BK), :] += grad_values

        return carry

    lax.fori_loop(0, blocks, step, 0)
    cosine, sine = cos_ref[...], sin_ref[...]
    half = HD // 2
    for h in range(heads):
        lower = acc_ref[h * HD : h * HD + half, :] * HD**-0.5
        upper = acc_ref[h * HD + half : (h + 1) * HD, :] * HD**-0.5
        dq_ref[h * HD : h * HD + half, :] = (lower * cosine + upper * sine).astype(BF16)
        dq_ref[h * HD + half : (h + 1) * HD, :] = (upper * cosine - lower * sine).astype(BF16)
    half_count = own_ref.shape[0]
    for ref, lo, more in ((own_ref, 0, refs[0]), (other_ref, half_count, refs[1])):
        made = beside([dk_ref[lo : lo + half_count, :], dv_ref[lo : lo + half_count, :]])
        ref[...] = made + more[...] if carried else made


def attend_back(flags, q_t, grad_t, o_t, lse, info, cosine_t, sine_t, keys, values, keys_t, codes, first, base, carry):
    width = q_t.shape[0]
    heads = width // HD
    count = keys.shape[0]
    blocks = count // BK
    whole = lambda i, f: (0, 0)
    column = lambda i, f: (0, base + first)
    pair = pl.BlockSpec((count // 2, 2 * HD), whole)
    return pl.pallas_call(
        functools.partial(attend_back_kernel, heads, blocks, first, carry is not None),
        out_shape=(
            jax.ShapeDtypeStruct((width, BQ), BF16),
            jax.ShapeDtypeStruct((count // 2, 2 * HD), F32),
            jax.ShapeDtypeStruct((count // 2, 2 * HD), F32),
        ),
        grid_spec=pltpu.PrefetchScalarGridSpec(
            num_scalar_prefetch=1,
            grid=(1,),
            in_specs=[
                pl.BlockSpec((width, BQ), column),
                pl.BlockSpec((width, BQ), lambda i, f: (0, first)),
                pl.BlockSpec((width, BQ), whole),
                pl.BlockSpec((heads, BQ), whole),
                pl.BlockSpec((2, BQ), column),
                pl.BlockSpec((HD // 2, BQ), column),
                pl.BlockSpec((HD // 2, BQ), column),
                pl.BlockSpec((count, HD), whole),
                pl.BlockSpec((count, HD), whole),
                pl.BlockSpec((HD, count), whole),
                pl.BlockSpec((count, 1), whole),
            ]
            + ([pair, pair] if carry is not None else []),
            out_specs=[pl.BlockSpec((width, BQ), whole), pair, pair],
            scratch_shapes=[
                pltpu.VMEM((width, BQ), F32),
                pltpu.VMEM((heads, BQ), F32),
                pltpu.VMEM((count, HD), F32),
                pltpu.VMEM((count, HD), F32),
            ],
        ),
        compiler_params=pltpu.CompilerParams(vmem_limit_bytes=32 << 20),
        cost_estimate=SMALL_COST,
        name="attend_back",
    )(flags, q_t, grad_t, o_t, lse, info, cosine_t, sine_t, keys, values, keys_t, codes, *(carry or ()))


def block_flags(codes, starts, key_codes):
    top = jnp.max(codes.reshape(-1, BQ), axis=1)
    low = jnp.min(starts.reshape(-1, BQ), axis=1)
    blocks = key_codes.reshape(-1, BK)
    key_low = jnp.min(blocks, axis=1)
    key_top = jnp.max(jnp.where(blocks < NEVER, blocks, -1), axis=1)
    seen = (key_low[None, :] <= top[:, None]) & (key_top[None, :] >= low[:, None])
    return seen.astype(jnp.int32).reshape(-1)


def rowwise_kernel(fn, bounds, lists, flats, consts, outs, choice, *refs):
    pieces = len(bounds)
    n_list = lists * pieces
    step = pl.program_id(0)
    flat_refs = refs[n_list : n_list + flats]
    const_refs = refs[n_list + flats : n_list + flats + consts]
    out_refs = refs[len(refs) - outs[0] - outs[1] : len(refs) - outs[1]]
    sum_refs = refs[len(refs) - outs[1] :]

    if outs[1]:
        @pl.when(step == 0)
        def _():
            for ref in sum_refs:
                ref[...] = jnp.zeros_like(ref)

    for j, (lo, hi) in enumerate(bounds):
        @pl.when((step >= lo) & (step < hi))
        def _():
            got, sums = fn(
                choice[0],
                [refs[k * pieces + j][...].astype(F32) for k in range(lists)],
                [ref[...].astype(F32) for ref in flat_refs],
                [ref[...] for ref in const_refs],
            )
            for ref, value in zip(out_refs, got):
                ref[...] = value.astype(ref.dtype)
            for ref, value in zip(sum_refs, sums):
                ref[...] += value


def tile_of(size):
    return next(tile for tile in (128, 160, 96, 64, 32, 16) if size % tile == 0)


def rowwise(fn, choice, lists, flats, consts, outs, sums=0, after=(), name="rowwise", into=None):
    tile = tile_of(lists[0][0].shape[0])
    sizes = [piece.shape[0] // tile for piece in lists[0]]
    width = lists[0][0].shape[1]
    bounds, lo = [], 0
    for size in sizes:
        bounds.append((lo, lo + size))
        lo += size
    total = lo

    def piece_map(lo, size):
        return lambda i, c: (jnp.clip(i - lo, 0, size - 1), 0)

    in_specs, operands = [], []
    for pieces in lists:
        for piece, (lo, hi) in zip(pieces, bounds):
            in_specs.append(pl.BlockSpec((tile, width), piece_map(lo, hi - lo)))
            operands.append(piece)
    for array, first in flats:
        offset = first // tile
        in_specs.append(pl.BlockSpec((tile, array.shape[1]), lambda i, c, offset=offset: (i + offset, 0)))
        operands.append(array)
    for array in consts:
        in_specs.append(pl.BlockSpec((1, array.shape[1]), lambda i, c: (0, 0)))
        operands.append(array)
    for array in after:
        in_specs.append(pl.BlockSpec(memory_space=pl.ANY))
        operands.append(array)
    rows = total * tile
    aliases, out_first, out_rows = {}, 0, rows
    if into is not None:
        held, out_first, out_rows = into
        if held is not None:
            aliases = {1 + len(operands): 0}
            in_specs.append(pl.BlockSpec(memory_space=pl.ANY))
            operands.append(held)
    shift = out_first // tile
    return pl.pallas_call(
        functools.partial(rowwise_kernel, fn, bounds, len(lists), len(flats), len(consts), (len(outs), sums)),
        out_shape=[jax.ShapeDtypeStruct((rows if n else out_rows, width), dtype) for n, dtype in enumerate(outs)]
        + [jax.ShapeDtypeStruct((1, width), F32)] * sums,
        grid_spec=pltpu.PrefetchScalarGridSpec(
            num_scalar_prefetch=1,
            grid=(total,),
            in_specs=in_specs,
            out_specs=[pl.BlockSpec((tile, width), lambda i, c, n=n: (i if n else i + shift, 0)) for n in range(len(outs))]
            + [pl.BlockSpec((1, width), lambda i, c: (0, 0))] * sums,
        ),
        compiler_params=pltpu.CompilerParams(vmem_limit_bytes=(60 if len(flats) > 1 else 32) << 20),
        cost_estimate=SMALL_COST,
        input_output_aliases=aliases,
        name=name,
    )(choice, *operands)


def add_fn(choice, lists, flats, consts):
    return [lists[0] + lists[1]], []


def pick(choice, total, third):
    return jnp.where(choice > 0, total, third)


def row_scale(values):
    return lax.rsqrt(jnp.mean(values * values, axis=1, keepdims=True) + EPS)


def middle_fn(choice, lists, flats, consts):
    branch = pick(choice, lists[0], lists[1])
    middle = flats[0] + branch
    return [branch, middle * row_scale(middle) * consts[0]], []


def column_sum(values):
    return jnp.sum(values, axis=0, keepdims=True)


def grad_middle_fn(choice, lists, flats, consts):
    grad = pick(choice, lists[0], lists[1])
    tokens, branch, seed, live = flats
    middle = tokens + branch
    scale = row_scale(middle)
    weighted = grad * consts[0]
    mean = jnp.mean(weighted * middle, axis=1, keepdims=True)
    out = seed * live + scale * weighted - middle * scale**3 * mean
    return [out, out], [column_sum(grad * middle * scale)]


def input_grad_fn(choice, lists, flats, consts):
    grad = pick(choice, lists[0], lists[1])
    tokens, grad_middle = flats
    scale = row_scale(tokens)
    weighted = grad * consts[0]
    mean = jnp.mean(weighted * tokens, axis=1, keepdims=True)
    return [grad_middle + scale * weighted - tokens * scale**3 * mean], []


def gain_fn(choice, lists, flats, consts):
    return [], [column_sum(lists[0] * flats[0] * row_scale(flats[0]))]


def result_fn(choice, lists, flats, consts):
    mlp_branch = pick(choice, lists[0], lists[1])
    tokens, branch, live = flats
    result = (tokens + branch + mlp_branch) * live
    return [result], [
        column_sum(result * result),
        column_sum(branch * branch * live),
        column_sum(mlp_branch * mlp_branch * live),
    ]


def pair_back_kernel(own_ref, returned_ref, cos_ref, sin_ref, out_ref):
    both = (own_ref[...] + returned_ref[...]).T
    half = HD // 2
    low, high = both[:half, :], both[half:HD, :]
    cosine, sine = cos_ref[...], sin_ref[...]
    out_ref[:half, :] = (low * cosine + high * sine).astype(BF16)
    out_ref[half:HD, :] = (high * cosine - low * sine).astype(BF16)
    out_ref[HD:, :] = both[HD:, :].astype(BF16)


def pair_back(own, returned, cosine_t, sine_t, block):
    rows = own.shape[0]
    whole = pl.BlockSpec((rows, 2 * HD), lambda i: (0, 0))
    table = pl.BlockSpec((HD // 2, rows), lambda i: (0, block))
    return pl.pallas_call(
        pair_back_kernel,
        out_shape=jax.ShapeDtypeStruct((2 * HD, rows), BF16),
        grid_spec=pltpu.PrefetchScalarGridSpec(
            num_scalar_prefetch=0,
            grid=(1,),
            in_specs=[whole, whole, table, table],
            out_specs=pl.BlockSpec((2 * HD, rows), lambda i: (0, 0)),
        ),
        cost_estimate=SMALL_COST,
        name="pair_back",
    )(own, returned, cosine_t, sine_t)


def send_in(part):
    return lax.ppermute(part, "tensor", [(0, 1), (3, 2)])


def send_across(pair):
    return lax.ppermute(pair, "tensor", [(1, 2), (2, 1)])


def send_out(total):
    return lax.ppermute(total, "tensor", [(1, 0), (2, 3)])


def held_back(value, dep):
    return value + dep[:1, :1].astype(F32) * 0.0


class Sums:
    def __init__(self, choice):
        self.choice = choice
        self.last = None
        self.order = []
        self.parts, self.firsts, self.pairs, self.seconds, self.totals, self.thirds = {}, {}, {}, {}, {}, {}

    def ordered(self, fn, *args, **more):
        after = tuple(more.pop("after", ()))
        held = more.get("into", (None,))[0]
        if self.last is not None and self.last is not held:
            after += (self.last,)
        got = rowwise(fn, self.choice, *args, after=after, **more)
        self.last = got[0]
        return got

    def ordered_sum(self, fn, lists, flats, name):
        got = rowwise(fn, self.choice, lists, flats, [], [], sums=1, after=(self.last,), name=name)
        self.last = got[0]
        return got[0]

    def push(self, k, part):
        self.order.append(k)
        self.parts[k] = part
        self.firsts[k] = send_in(part)

    def pair(self, k, after=()):
        spot = self.order.index(k)
        if spot == 3:
            after = tuple(after) + (self.thirds[self.order[0]],)
        both = [[self.parts[k]], [self.firsts[k]]]
        self.pairs[k] = self.ordered(add_fn, both, [], [], [BF16], after=after, name="pair")[0]
        self.seconds[k] = send_across(self.pairs[k])

    def total(self, k, after=()):
        both = [[self.pairs[k]], [self.seconds[k]]]
        self.totals[k] = self.ordered(add_fn, both, [], [], [BF16], after=after, name="total")[0]
        self.thirds[k] = send_out(self.totals[k])

    def of(self, picked):
        return [self.totals[k] for k in picked], [self.thirds[k] for k in picked]


def small_sum(part):
    part = part + lax.ppermute(part, "tensor", [(0, 1), (1, 0), (2, 3), (3, 2)])
    return part + lax.ppermute(part, "tensor", [(0, 2), (2, 0), (1, 3), (3, 1)])


def gather_rows(shard):
    return lax.all_gather(shard, ROW_AXES, axis=0, tiled=True)


def same(ref, *rest):
    pass


def once(value, after):
    anywhere = pl.BlockSpec(memory_space=pl.ANY)
    return pl.pallas_call(
        same,
        out_shape=jax.ShapeDtypeStruct(value.shape, value.dtype),
        in_specs=[anywhere] * (1 + len(after)),
        out_specs=anywhere,
        input_output_aliases={0: 0},
        cost_estimate=SMALL_COST,
        name="once",
    )(value, *after)


def scatter_rows(grads):
    return lax.psum_scatter(grads, ROW_AXES, scatter_dimension=0, tiled=True).astype(F32)


def fold(values, row_count):
    return jnp.broadcast_to(values, (row_count,)).astype(BF16)[:, None]


def spread_small(values):
    size = lax.axis_size("dp")
    step = 1
    while step < size:
        values = values + lax.ppermute(values, "dp", [(i, i ^ step) for i in range(size)])
        step *= 2
    return values + lax.ppermute(values, "ctx", [(0, 1), (1, 0)])


def body(hidden_in, lengths, w_query, w_keyval, w_output, w_gateup, w_down, gain_attn, gain_mlp, cotangent):
    micro, span, width = hidden_in.shape
    rows = micro * span
    shard_rows = w_query.shape[0]
    q_width = w_query.shape[1]
    ff = w_down.shape[1]
    heads = q_width // HD
    half = HD // 2
    here = lax.axis_index("ctx")
    place = lax.axis_index("tensor")
    choice = ((place == 1) | (place == 2)).astype(jnp.int32).reshape(1)
    sums = Sums(choice)
    join = lambda parts: jnp.concatenate(parts, axis=0)

    gains = jnp.stack([gain_attn, gain_mlp], axis=1)
    gains = jnp.pad(gains, ((0, 0), (0, 126)))
    packed = jnp.concatenate([w_query, w_keyval.reshape(shard_rows, -1), gains], axis=1)
    first = gather_rows(packed)
    qkv_w = first[:, : q_width + 2 * HD]
    gain_pair = first[:, q_width + 2 * HD : q_width + 2 * HD + 2].astype(F32).T
    attn_gain, mlp_gain = gain_pair[0:1], gain_pair[1:2]
    output_w = gather_rows(w_output)
    gateup_w = gather_rows(w_gateup.reshape(shard_rows, 2 * ff))
    down_w = gather_rows(w_down)

    slot_lengths = lax.dynamic_slice_in_dim(lengths, lax.axis_index("dp") * micro, micro)
    slot_of = jnp.repeat(jnp.arange(micro, dtype=jnp.int32), span)
    length_of = jnp.repeat(slot_lengths, span)
    offset = jnp.tile(jnp.arange(span, dtype=jnp.int32), micro)
    position = here * span + offset
    other_position = (1 - here) * span + offset
    live = (position < length_of).astype(F32)[:, None]
    starts = slot_of * SLOT_STEP
    codes = starts + position
    own_codes = jnp.where(position < length_of, codes, NEVER)
    other_codes = jnp.where(other_position < length_of, starts + other_position, NEVER)
    info = jnp.stack([codes, starts])

    frequency = THETA ** (-jnp.arange(0, HD, 2).astype(F32) / HD)
    angles = position.astype(F32)[:, None] * frequency[None, :]
    cosine, sine = jnp.cos(angles), jnp.sin(angles)
    cosine_t, sine_t = cosine.T, sine.T

    hidden_flat = hidden_in.reshape(rows, width)
    seed_flat = cotangent.reshape(rows, width)
    tokens = hidden_flat.astype(F32)

    attn_scale = rms_scale(tokens)
    normed = (tokens * attn_scale * attn_gain).astype(BF16)
    kv_lin = dot(normed, qkv_w[:, q_width:], 1, 0)
    k_low, k_high = kv_lin[:, :half], kv_lin[:, half:HD]
    own_pair = jnp.concatenate(
        [k_low * cosine - k_high * sine, k_high * cosine + k_low * sine, kv_lin[:, HD:]], axis=1
    ).astype(BF16)
    other_pair = lax.ppermute(own_pair, "ctx", [(0, 1), (1, 0)])
    q_lin = dot(qkv_w[:, :q_width], normed, 0, 1).reshape(heads, 2, half, rows) * HD**-0.5
    q_t = jnp.stack(
        [
            q_lin[:, 0] * cosine_t - q_lin[:, 1] * sine_t,
            q_lin[:, 1] * cosine_t + q_lin[:, 0] * sine_t,
        ],
        axis=1,
    ).astype(BF16).reshape(q_width, rows)

    chunk = span // 2
    one, two = slice(0, span), slice(span, 2 * span)
    groups = []
    for at in (one, two):
        pairs = join([own_pair[at], other_pair[at]])
        pairs_t = pairs.T
        key_codes = join([own_codes[at], other_codes[at]])
        groups.append(
            dict(
                flags=block_flags(codes[at], starts[at], key_codes),
                keys=pairs[:, :HD],
                values=pairs[:, HD:],
                keys_t=pairs_t[:HD],
                values_t=pairs_t[HD:],
                codes=key_codes[:, None],
                context=[],
                lse=[],
            )
        )

    def attend_chunk(group, k):
        g = groups[group]
        context, lse = attend(
            g["flags"], q_t, info, g["keys"], g["values_t"], g["codes"], k, group * span // BQ, chunk // BQ
        )
        g["context"].append(context)
        g["lse"].append(lse)
        return dot(context, output_w, 0, 1)

    def push(k, part, size=chunk):
        for n in range(part.shape[0] // size):
            sums.push(k + n, part[n * size : (n + 1) * size].astype(BF16))

    push(0, attend_chunk(0, 0))
    push(1, attend_chunk(0, 1))
    push(2, attend_chunk(1, 0))
    sums.pair(0, (sums.parts[2],))
    push(3, attend_chunk(1, 1))
    sums.pair(1, (sums.parts[3],))
    sums.total(0)
    sums.pair(2)
    sums.total(1)
    sums.pair(3)
    sums.total(2)

    def middle_of(first, at, after=()):
        return sums.ordered(
            middle_fn, sums.of([first, first + 1]), [(hidden_flat, at.start)], [mlp_gain], [BF16, BF16], after=after, name="middle"
        )

    def forward(normed_rows):
        return dot(normed_rows, gateup_w, 1, 0)

    def products(gateup, seed_rows):
        grad_hidden = dot(seed_rows, down_w, 1, 0)
        gate, up = gateup[:, :ff], gateup[:, ff:]
        sigma = jax.nn.sigmoid(gate)
        activated = gate * sigma
        grad_gate = grad_hidden * up * (sigma * (1.0 + gate * (1.0 - sigma)))
        return (activated * up).astype(BF16), jnp.concatenate([grad_gate, grad_hidden * activated], axis=1).astype(BF16)

    mlp_seed = (seed_flat.astype(F32) * live).astype(BF16)
    attn_out_one, normed_one = middle_of(0, one)
    gateup = forward(normed_one)
    sums.total(3, (gateup,))
    hidden_one, grad_gateup_one = products(gateup, mlp_seed[one])
    push(4, dot(grad_gateup_one, gateup_w, 1, 1))
    attn_out_two, normed_two = middle_of(2, two, (sums.parts[5],))
    gateup = forward(normed_two)
    sums.pair(4, (gateup,))
    hidden_two, grad_gateup_two = products(gateup, mlp_seed[two])
    push(6, held_back(dot(grad_gateup_two, gateup_w, 1, 1), sums.last))
    sums.pair(5, (sums.parts[7],))
    sums.total(4)
    hidden = join([hidden_one, hidden_two])
    push(8, held_back(dot(hidden_one, down_w, 1, 1), sums.last), span)
    push(10, held_back(dot(hidden_two, down_w, 1, 1), sums.parts[8]), span)
    sums.pair(6, (sums.parts[10], sums.thirds[4]))
    sums.total(5)
    grad_gateup_w = held_back(
        dot(join([normed_one, normed_two]), join([grad_gateup_one, grad_gateup_two]), 0, 0), sums.last
    ).astype(BF16)
    sums.pair(7, (grad_gateup_w, sums.thirds[5]))
    sums.total(6)
    grad_gateup_w = scatter_rows(once(grad_gateup_w, (sums.totals[6],)))

    def grad_middle_of(first, at, attn_out, after=()):
        return sums.ordered(
            grad_middle_fn,
            sums.of([first, first + 1]),
            [(hidden_flat, at.start), (attn_out, 0), (seed_flat, at.start), (live, at.start)],
            [mlp_gain],
            [F32, BF16],
            sums=1,
            after=after,
            name="grad_middle",
        )

    def attend_back_group(group, seeds):
        g = groups[group]
        grad_context_t = held_back(dot(output_w, seeds, 0, 1), sums.last).astype(BF16)
        carry, grads = None, []
        for k in range(2):
            grad_q, *carry = attend_back(
                g["flags"], q_t, grad_context_t, g["context"][k], g["lse"][k], info, cosine_t, sine_t,
                g["keys"], g["values"], g["keys_t"], g["codes"], k, group * span // BQ, carry,
            )
            grads.append(grad_q)
        returned = lax.ppermute(carry[1], "ctx", [(0, 1), (1, 0)])
        grad_pair = pair_back(carry[0], returned, cosine_t, sine_t, group)
        g["grad"] = jnp.concatenate([jnp.concatenate(grads, axis=1), grad_pair], axis=0)
        return grads[1]

    def attn_back_of(group):
        return dot(groups[group]["grad"], qkv_w, 0, 1)

    grad_middle_one, attn_seed_one, gain_mlp_one = grad_middle_of(4, one, attn_out_one)
    sums.total(7, (sums.thirds[6],))
    done = attend_back_group(0, attn_seed_one)
    sums.pair(8, (done,))
    grad_middle_two, attn_seed_two, gain_mlp_two = grad_middle_of(6, two, attn_out_two)
    push(12, held_back(attn_back_of(0), sums.last))
    done = attend_back_group(1, attn_seed_two)
    sums.pair(10, (done, sums.parts[13]))
    sums.total(8)
    grad_down = held_back(dot(mlp_seed, hidden, 0, 0), sums.last).astype(BF16)
    push(14, held_back(attn_back_of(1), grad_down))
    sums.pair(12, (sums.parts[15],))
    sums.pair(13, (sums.thirds[8],))
    sums.total(10)
    grad_down = scatter_rows(once(grad_down, (sums.totals[10], grad_gateup_w)))
    sums.total(12)
    gain_attn_part = sums.ordered_sum(
        gain_fn, [[sums.parts[12 + k] for k in range(4)]], [(hidden_flat, 0)], "gain_attn"
    )
    extra = jnp.concatenate([fold(gain_attn_part[0], width), fold((gain_mlp_one + gain_mlp_two)[0], width)], axis=1)
    extra = jnp.pad(extra, ((0, 0), (0, 126)))
    grad_qkv_t = jnp.concatenate([groups[0]["grad"], groups[1]["grad"]], axis=1)
    context_t = jnp.concatenate(groups[0]["context"] + groups[1]["context"], axis=1)
    last = jnp.concatenate(
        [
            held_back(dot(normed, grad_qkv_t, 0, 1), sums.last).astype(BF16),
            extra,
            held_back(dot(join([attn_seed_one, attn_seed_two]), context_t, 0, 1), sums.last).astype(BF16),
        ],
        axis=1,
    )

    def result_of(first, at, attn_out, held, after=()):
        return sums.ordered(
            result_fn,
            sums.of([first]),
            [(hidden_flat, at.start), (attn_out, 0), (live, at.start)],
            [],
            [BF16],
            sums=3,
            after=after,
            into=(held, at.start, rows),
            name="result",
        )

    def input_grad_of(first, at, grad_middle, held, after=()):
        return sums.ordered(
            input_grad_fn,
            sums.of([first, first + 1]),
            [(hidden_flat, at.start), (grad_middle, 0)],
            [attn_gain],
            [BF16],
            after=after,
            into=(held, at.start, rows),
            name="input_grad",
        )[0]

    sums.pair(14, (last,))
    sums.total(13)
    sums.pair(15, (sums.thirds[10],))
    sums.total(14)
    sums.total(15, (sums.thirds[12],))
    last = scatter_rows(once(last, (sums.totals[15], grad_down)))
    output, *squares_one = result_of(8, one, attn_out_one, None)
    output, *squares_two = result_of(10, two, attn_out_two, output)
    grad_gateup_w = grad_gateup_w.reshape(w_gateup.shape)
    input_grad = input_grad_of(12, one, grad_middle_one, None)
    input_grad = input_grad_of(14, two, grad_middle_two, input_grad, (grad_gateup_w, grad_down))
    squares = [jnp.sum(x) + jnp.sum(y) for x, y in zip(squares_one, squares_two)]
    squares = spread_small(jnp.broadcast_to(jnp.stack(squares + [0.0])[None, :], (8, 4)))[0, :3]
    root_means = jnp.sqrt(squares / (jnp.sum(lengths).astype(F32) * width))
    at = q_width + 2 * HD
    return (
        output.reshape(hidden_in.shape),
        input_grad.reshape(hidden_in.shape),
        last[:, :q_width],
        last[:, q_width:at].reshape(w_keyval.shape),
        last[:, at + 128 :],
        grad_gateup_w,
        grad_down,
        small_sum(last[:, at]),
        last[:, at + 1],
        root_means,
    )


def solution(mesh):
    placed = (
        P("dp", "ctx", None),
        P(),
        P(("dp", "ctx"), "tensor"),
        P(("dp", "ctx"), "tensor", None),
        P(("dp", "ctx"), "tensor"),
        P(("dp", "ctx"), None, "tensor"),
        P(("dp", "ctx"), "tensor"),
        P(("dp", "ctx")),
        P(("dp", "ctx")),
        P("dp", "ctx", None),
    )
    return jax.shard_map(
        body,
        mesh=mesh,
        in_specs=placed,
        out_specs=(
            P("dp", "ctx", None),
            P("dp", "ctx", None),
            P(("dp", "ctx"), "tensor"),
            P(("dp", "ctx"), "tensor", None),
            P(("dp", "ctx"), "tensor"),
            P(("dp", "ctx"), None, "tensor"),
            P(("dp", "ctx"), "tensor"),
            P(("dp", "ctx")),
            P(("dp", "ctx")),
            P(),
        ),
        check_vma=False,
    )
```

```python
import functools

import jax
import jax.numpy as jnp
from jax import lax
from jax.experimental import pallas as pl
from jax.experimental.pallas import tpu as pltpu
from jax.sharding import PartitionSpec as P

HD = 64
EPS = 1e-05
THETA = 10000.0
NEG_FILL = -1e30
SLOT_STEP = 1 << 16
NEVER = 1 << 30
BQ = 256
BK = 256
SIDE = 1
F32 = jnp.float32
BF16 = jnp.bfloat16
SMALL_COST = pl.CostEstimate(flops=1024, bytes_accessed=1024, transcendentals=0)
ROW_AXES = ("dp", "ctx")


def dot(left, right, left_dim, right_dim):
    return lax.dot_general(
        left, right, (((left_dim,), (right_dim,)), ((), ())), preferred_element_type=F32
    )


def rms_scale(values):
    return lax.rsqrt(jnp.mean(values * values, axis=-1, keepdims=True) + EPS)


def mask_bias(key_code, query_info):
    code, start = query_info[0:1, :], query_info[1:2, :]
    allowed = (key_code <= code) & (key_code >= start)
    return jnp.where(allowed, 0.0, NEG_FILL)


def beside(parts):
    return jnp.concatenate(parts, axis=1)


def heads_of(ref, rows):
    return beside([ref[r * HD : (r + 1) * HD, :] for r in rows])


def rows_of(ref, rows):
    return beside([ref[r : r + 1, :] for r in rows])


def attend_kernel(heads, blocks, first, flags, q_ref, info_ref, k_ref, vt_ref, code_ref, o_ref, lse_ref, m_ref, l_ref, acc_ref):
    m_ref[...] = jnp.full_like(m_ref, NEG_FILL)
    l_ref[...] = jnp.zeros_like(l_ref)
    acc_ref[...] = jnp.zeros_like(acc_ref)
    row = first + pl.program_id(0)

    def step(kb, carry):
        @pl.when(flags[row * blocks + kb] > 0)
        def _():
            at = pl.multiple_of(kb * BK, BK)
            keys = k_ref[pl.ds(at, BK), :]
            values_t = vt_ref[:, pl.ds(at, BK)]
            bias = beside([mask_bias(code_ref[pl.ds(at, BK), :], info_ref[...])] * SIDE)
            for h in range(0, heads, SIDE):
                rows = range(h, h + SIDE)
                scores = dot(keys, heads_of(q_ref, rows), 1, 0) + bias
                before = rows_of(m_ref, rows)
                top = jnp.maximum(before, jnp.max(scores, axis=0, keepdims=True))
                shrink = jnp.exp(before - top)
                weights = jnp.exp(scores - top)
                total = shrink * rows_of(l_ref, rows) + jnp.sum(weights, axis=0, keepdims=True)
                out = shrink * heads_of(acc_ref, rows) + dot(values_t, weights.astype(BF16), 1, 0)
                for n, r in enumerate(rows):
                    lanes = slice(n * BQ, (n + 1) * BQ)
                    m_ref[r : r + 1, :] = top[:, lanes]
                    l_ref[r : r + 1, :] = total[:, lanes]
                    acc_ref[r * HD : (r + 1) * HD, :] = out[:, lanes]

        return carry

    lax.fori_loop(0, blocks, step, 0)
    total = l_ref[...]
    total = jnp.where(total == 0.0, 1.0, total)
    lse_ref[...] = m_ref[...] + jnp.log(total)
    for h in range(heads):
        part = slice(h * HD, (h + 1) * HD)
        o_ref[part, :] = (acc_ref[part, :] / total[h : h + 1, :]).astype(BF16)


def attend(flags, q_t, info, keys, values_t, codes, first, base, steps):
    width = q_t.shape[0]
    rows = steps * BQ
    heads = width // HD
    count = keys.shape[0]
    blocks = count // BK
    whole = lambda i, f: (0, 0)
    column = lambda i, f: (0, base + first + i)
    made = lambda i, f: (0, i)
    return pl.pallas_call(
        functools.partial(attend_kernel, heads, blocks, first),
        out_shape=(
            jax.ShapeDtypeStruct((width, rows), BF16),
            jax.ShapeDtypeStruct((heads, rows), F32),
        ),
        grid_spec=pltpu.PrefetchScalarGridSpec(
            num_scalar_prefetch=1,
            grid=(steps,),
            in_specs=[
                pl.BlockSpec((width, BQ), column),
                pl.BlockSpec((2, BQ), column),
                pl.BlockSpec((count, HD), whole),
                pl.BlockSpec((HD, count), whole),
                pl.BlockSpec((count, 1), whole),
            ],
            out_specs=[pl.BlockSpec((width, BQ), made), pl.BlockSpec((heads, BQ), made)],
            scratch_shapes=[
                pltpu.VMEM((heads, BQ), F32),
                pltpu.VMEM((heads, BQ), F32),
                pltpu.VMEM((width, BQ), F32),
            ],
        ),
        compiler_params=pltpu.CompilerParams(vmem_limit_bytes=24 << 20),
        cost_estimate=SMALL_COST,
        name="attend",
    )(flags, q_t, info, keys, values_t, codes)


def attend_back_kernel(
    heads, blocks, first, carried, flags, q_ref, do_ref, o_ref, lse_ref, info_ref, cos_ref, sin_ref, k_ref, v_ref, kt_ref,
    code_ref, *refs
):
    row = first
    dq_ref, own_ref, other_ref, acc_ref, delta_ref, dk_ref, dv_ref = refs[-7:]
    dk_ref[...] = jnp.zeros_like(dk_ref)
    dv_ref[...] = jnp.zeros_like(dv_ref)

    acc_ref[...] = jnp.zeros_like(acc_ref)
    for h in range(heads):
        part = slice(h * HD, (h + 1) * HD)
        delta_ref[h : h + 1, :] = jnp.sum(
            do_ref[part, :].astype(F32) * o_ref[part, :].astype(F32), axis=0, keepdims=True
        )

    def step(kb, carry):
        @pl.when(flags[row * blocks + kb] > 0)
        def _():
            at = pl.multiple_of(kb * BK, BK)
            keys = k_ref[pl.ds(at, BK), :]
            values = v_ref[pl.ds(at, BK), :]
            keys_t = kt_ref[:, pl.ds(at, BK)]
            bias = beside([mask_bias(code_ref[pl.ds(at, BK), :], info_ref[...])] * SIDE)
            grad_keys = jnp.zeros((BK, HD), F32)
            grad_values = jnp.zeros((BK, HD), F32)
            for h in range(0, heads, SIDE):
                rows = range(h, h + SIDE)
                queries = heads_of(q_ref, rows)
                grads = heads_of(do_ref, rows)
                weights = jnp.exp(dot(keys, queries, 1, 0) + bias - rows_of(lse_ref, rows))
                grad_weights = dot(values, grads, 1, 0)
                raw = (weights * (grad_weights - rows_of(delta_ref, rows))).astype(BF16)
                grad_values = grad_values + dot(weights.astype(BF16), grads, 1, 1)
                grad_keys = grad_keys + dot(raw, queries, 1, 1)
                out = dot(keys_t, raw, 1, 0)
                for n, r in enumerate(rows):
                    acc_ref[r * HD : (r + 1) * HD, :] += out[:, n * BQ : (n + 1) * BQ]
            dk_ref[pl.ds(at, BK), :] += grad_keys
            dv_ref[pl.ds(at, BK), :] += grad_values

        return carry

    lax.fori_loop(0, blocks, step, 0)
    cosine, sine = cos_ref[...], sin_ref[...]
    half = HD // 2
    for h in range(heads):
        lower = acc_ref[h * HD : h * HD + half, :] * HD**-0.5
        upper = acc_ref[h * HD + half : (h + 1) * HD, :] * HD**-0.5
        dq_ref[h * HD : h * HD + half, :] = (lower * cosine + upper * sine).astype(BF16)
        dq_ref[h * HD + half : (h + 1) * HD, :] = (upper * cosine - lower * sine).astype(BF16)
    half_count = own_ref.shape[0]
    for ref, lo, more in ((own_ref, 0, refs[0]), (other_ref, half_count, refs[1])):
        made = beside([dk_ref[lo : lo + half_count, :], dv_ref[lo : lo + half_count, :]])
        ref[...] = made + more[...] if carried else made


def attend_back(flags, q_t, grad_t, o_t, lse, info, cosine_t, sine_t, keys, values, keys_t, codes, first, base, carry):
    width = q_t.shape[0]
    heads = width // HD
    count = keys.shape[0]
    blocks = count // BK
    whole = lambda i, f: (0, 0)
    column = lambda i, f: (0, base + first)
    pair = pl.BlockSpec((count // 2, 2 * HD), whole)
    return pl.pallas_call(
        functools.partial(attend_back_kernel, heads, blocks, first, carry is not None),
        out_shape=(
            jax.ShapeDtypeStruct((width, BQ), BF16),
            jax.ShapeDtypeStruct((count // 2, 2 * HD), F32),
            jax.ShapeDtypeStruct((count // 2, 2 * HD), F32),
        ),
        grid_spec=pltpu.PrefetchScalarGridSpec(
            num_scalar_prefetch=1,
            grid=(1,),
            in_specs=[
                pl.BlockSpec((width, BQ), column),
                pl.BlockSpec((width, BQ), lambda i, f: (0, first)),
                pl.BlockSpec((width, BQ), whole),
                pl.BlockSpec((heads, BQ), whole),
                pl.BlockSpec((2, BQ), column),
                pl.BlockSpec((HD // 2, BQ), column),
                pl.BlockSpec((HD // 2, BQ), column),
                pl.BlockSpec((count, HD), whole),
                pl.BlockSpec((count, HD), whole),
                pl.BlockSpec((HD, count), whole),
                pl.BlockSpec((count, 1), whole),
            ]
            + ([pair, pair] if carry is not None else []),
            out_specs=[pl.BlockSpec((width, BQ), whole), pair, pair],
            scratch_shapes=[
                pltpu.VMEM((width, BQ), F32),
                pltpu.VMEM((heads, BQ), F32),
                pltpu.VMEM((count, HD), F32),
                pltpu.VMEM((count, HD), F32),
            ],
        ),
        compiler_params=pltpu.CompilerParams(vmem_limit_bytes=32 << 20),
        cost_estimate=SMALL_COST,
        name="attend_back",
    )(flags, q_t, grad_t, o_t, lse, info, cosine_t, sine_t, keys, values, keys_t, codes, *(carry or ()))


def block_flags(codes, starts, key_codes):
    top = jnp.max(codes.reshape(-1, BQ), axis=1)
    low = jnp.min(starts.reshape(-1, BQ), axis=1)
    blocks = key_codes.reshape(-1, BK)
    key_low = jnp.min(blocks, axis=1)
    key_top = jnp.max(jnp.where(blocks < NEVER, blocks, -1), axis=1)
    seen = (key_low[None, :] <= top[:, None]) & (key_top[None, :] >= low[:, None])
    return seen.astype(jnp.int32).reshape(-1)


def rowwise_kernel(fn, bounds, lists, flats, consts, outs, choice, *refs):
    pieces = len(bounds)
    n_list = lists * pieces
    step = pl.program_id(0)
    flat_refs = refs[n_list : n_list + flats]
    const_refs = refs[n_list + flats : n_list + flats + consts]
    out_refs = refs[len(refs) - outs[0] - outs[1] : len(refs) - outs[1]]
    sum_refs = refs[len(refs) - outs[1] :]

    if outs[1]:
        @pl.when(step == 0)
        def _():
            for ref in sum_refs:
                ref[...] = jnp.zeros_like(ref)

    for j, (lo, hi) in enumerate(bounds):
        @pl.when((step >= lo) & (step < hi))
        def _():
            got, sums = fn(
                choice[0],
                [refs[k * pieces + j][...].astype(F32) for k in range(lists)],
                [ref[...].astype(F32) for ref in flat_refs],
                [ref[...] for ref in const_refs],
            )
            for ref, value in zip(out_refs, got):
                ref[...] = value.astype(ref.dtype)
            for ref, value in zip(sum_refs, sums):
                ref[...] += value


def tile_of(size):
    return next(tile for tile in (128, 160, 96, 64, 32, 16) if size % tile == 0)


def rowwise(fn, choice, lists, flats, consts, outs, sums=0, after=(), name="rowwise", into=None):
    tile = tile_of(lists[0][0].shape[0])
    sizes = [piece.shape[0] // tile for piece in lists[0]]
    width = lists[0][0].shape[1]
    bounds, lo = [], 0
    for size in sizes:
        bounds.append((lo, lo + size))
        lo += size
    total = lo

    def piece_map(lo, size):
        return lambda i, c: (jnp.clip(i - lo, 0, size - 1), 0)

    in_specs, operands = [], []
    for pieces in lists:
        for piece, (lo, hi) in zip(pieces, bounds):
            in_specs.append(pl.BlockSpec((tile, width), piece_map(lo, hi - lo)))
            operands.append(piece)
    for array, first in flats:
        offset = first // tile
        in_specs.append(pl.BlockSpec((tile, array.shape[1]), lambda i, c, offset=offset: (i + offset, 0)))
        operands.append(array)
    for array in consts:
        in_specs.append(pl.BlockSpec((1, array.shape[1]), lambda i, c: (0, 0)))
        operands.append(array)
    for array in after:
        in_specs.append(pl.BlockSpec(memory_space=pl.ANY))
        operands.append(array)
    rows = total * tile
    aliases, out_first, out_rows = {}, 0, rows
    if into is not None:
        held, out_first, out_rows = into
        if held is not None:
            aliases = {1 + len(operands): 0}
            in_specs.append(pl.BlockSpec(memory_space=pl.ANY))
            operands.append(held)
    shift = out_first // tile
    return pl.pallas_call(
        functools.partial(rowwise_kernel, fn, bounds, len(lists), len(flats), len(consts), (len(outs), sums)),
        out_shape=[jax.ShapeDtypeStruct((rows if n else out_rows, width), dtype) for n, dtype in enumerate(outs)]
        + [jax.ShapeDtypeStruct((1, width), F32)] * sums,
        grid_spec=pltpu.PrefetchScalarGridSpec(
            num_scalar_prefetch=1,
            grid=(total,),
            in_specs=in_specs,
            out_specs=[pl.BlockSpec((tile, width), lambda i, c, n=n: (i if n else i + shift, 0)) for n in range(len(outs))]
            + [pl.BlockSpec((1, width), lambda i, c: (0, 0))] * sums,
        ),
        compiler_params=pltpu.CompilerParams(vmem_limit_bytes=(60 if len(flats) > 1 else 32) << 20),
        cost_estimate=SMALL_COST,
        input_output_aliases=aliases,
        name=name,
    )(choice, *operands)


def add_fn(choice, lists, flats, consts):
    return [lists[0] + lists[1]], []


def pick(choice, total, third):
    return jnp.where(choice > 0, total, third)


def row_scale(values):
    return lax.rsqrt(jnp.mean(values * values, axis=1, keepdims=True) + EPS)


def middle_fn(choice, lists, flats, consts):
    branch = pick(choice, lists[0], lists[1])
    middle = flats[0] + branch
    return [branch, middle * row_scale(middle) * consts[0]], []


def column_sum(values):
    return jnp.sum(values, axis=0, keepdims=True)


def grad_middle_fn(choice, lists, flats, consts):
    grad = pick(choice, lists[0], lists[1])
    tokens, branch, seed, live = flats
    middle = tokens + branch
    scale = row_scale(middle)
    weighted = grad * consts[0]
    mean = jnp.mean(weighted * middle, axis=1, keepdims=True)
    out = seed * live + scale * weighted - middle * scale**3 * mean
    return [out, out], [column_sum(grad * middle * scale)]


def input_grad_fn(choice, lists, flats, consts):
    grad = pick(choice, lists[0], lists[1])
    tokens, grad_middle = flats
    scale = row_scale(tokens)
    weighted = grad * consts[0]
    mean = jnp.mean(weighted * tokens, axis=1, keepdims=True)
    return [grad_middle + scale * weighted - tokens * scale**3 * mean], []


def gain_fn(choice, lists, flats, consts):
    return [], [column_sum(lists[0] * flats[0] * row_scale(flats[0]))]


def result_fn(choice, lists, flats, consts):
    mlp_branch = pick(choice, lists[0], lists[1])
    tokens, branch, live = flats
    result = (tokens + branch + mlp_branch) * live
    return [result], [
        column_sum(result * result),
        column_sum(branch * branch * live),
        column_sum(mlp_branch * mlp_branch * live),
    ]


def pair_back_kernel(own_ref, returned_ref, cos_ref, sin_ref, out_ref):
    both = (own_ref[...] + returned_ref[...]).T
    half = HD // 2
    low, high = both[:half, :], both[half:HD, :]
    cosine, sine = cos_ref[...], sin_ref[...]
    out_ref[:half, :] = (low * cosine + high * sine).astype(BF16)
    out_ref[half:HD, :] = (high * cosine - low * sine).astype(BF16)
    out_ref[HD:, :] = both[HD:, :].astype(BF16)


def pair_back(own, returned, cosine_t, sine_t, block):
    rows = own.shape[0]
    whole = pl.BlockSpec((rows, 2 * HD), lambda i: (0, 0))
    table = pl.BlockSpec((HD // 2, rows), lambda i: (0, block))
    return pl.pallas_call(
        pair_back_kernel,
        out_shape=jax.ShapeDtypeStruct((2 * HD, rows), BF16),
        grid_spec=pltpu.PrefetchScalarGridSpec(
            num_scalar_prefetch=0,
            grid=(1,),
            in_specs=[whole, whole, table, table],
            out_specs=pl.BlockSpec((2 * HD, rows), lambda i: (0, 0)),
        ),
        cost_estimate=SMALL_COST,
        name="pair_back",
    )(own, returned, cosine_t, sine_t)


def send_in(part):
    return lax.ppermute(part, "tensor", [(0, 1), (3, 2)])


def send_across(pair):
    return lax.ppermute(pair, "tensor", [(1, 2), (2, 1)])


def send_out(total):
    return lax.ppermute(total, "tensor", [(1, 0), (2, 3)])


def held_back(value, dep):
    return value + dep[:1, :1].astype(F32) * 0.0


class Sums:
    def __init__(self, choice):
        self.choice = choice
        self.last = None
        self.order = []
        self.parts, self.firsts, self.pairs, self.seconds, self.totals, self.thirds = {}, {}, {}, {}, {}, {}

    def ordered(self, fn, *args, **more):
        after = tuple(more.pop("after", ()))
        held = more.get("into", (None,))[0]
        if self.last is not None and self.last is not held:
            after += (self.last,)
        got = rowwise(fn, self.choice, *args, after=after, **more)
        self.last = got[0]
        return got

    def ordered_sum(self, fn, lists, flats, name):
        got = rowwise(fn, self.choice, lists, flats, [], [], sums=1, after=(self.last,), name=name)
        self.last = got[0]
        return got[0]

    def push(self, k, part):
        self.order.append(k)
        self.parts[k] = part
        self.firsts[k] = send_in(part)

    def pair(self, k, after=()):
        spot = self.order.index(k)
        if spot == 3:
            after = tuple(after) + (self.thirds[self.order[0]],)
        both = [[self.parts[k]], [self.firsts[k]]]
        self.pairs[k] = self.ordered(add_fn, both, [], [], [BF16], after=after, name="pair")[0]
        self.seconds[k] = send_across(self.pairs[k])

    def total(self, k, after=()):
        both = [[self.pairs[k]], [self.seconds[k]]]
        self.totals[k] = self.ordered(add_fn, both, [], [], [BF16], after=after, name="total")[0]
        self.thirds[k] = send_out(self.totals[k])

    def of(self, picked):
        return [self.totals[k] for k in picked], [self.thirds[k] for k in picked]


def small_sum(part):
    part = part + lax.ppermute(part, "tensor", [(0, 1), (1, 0), (2, 3), (3, 2)])
    return part + lax.ppermute(part, "tensor", [(0, 2), (2, 0), (1, 3), (3, 1)])


def gather_rows(shard):
    return lax.all_gather(shard, ROW_AXES, axis=0, tiled=True)


def same(ref, *rest):
    pass


def once(value, after):
    anywhere = pl.BlockSpec(memory_space=pl.ANY)
    return pl.pallas_call(
        same,
        out_shape=jax.ShapeDtypeStruct(value.shape, value.dtype),
        in_specs=[anywhere] * (1 + len(after)),
        out_specs=anywhere,
        input_output_aliases={0: 0},
        cost_estimate=SMALL_COST,
        name="once",
    )(value, *after)


def scatter_rows(grads):
    return lax.psum_scatter(grads, ROW_AXES, scatter_dimension=0, tiled=True).astype(F32)


def fold(values, row_count):
    return jnp.broadcast_to(values, (row_count,)).astype(BF16)[:, None]


def spread_small(values):
    size = lax.axis_size("dp")
    step = 1
    while step < size:
        values = values + lax.ppermute(values, "dp", [(i, i ^ step) for i in range(size)])
        step *= 2
    return values + lax.ppermute(values, "ctx", [(0, 1), (1, 0)])


def body(hidden_in, lengths, w_query, w_keyval, w_output, w_gateup, w_down, gain_attn, gain_mlp, cotangent):
    micro, span, width = hidden_in.shape
    rows = micro * span
    shard_rows = w_query.shape[0]
    q_width = w_query.shape[1]
    ff = w_down.shape[1]
    heads = q_width // HD
    half = HD // 2
    here = lax.axis_index("ctx")
    place = lax.axis_index("tensor")
    choice = ((place == 1) | (place == 2)).astype(jnp.int32).reshape(1)
    sums = Sums(choice)
    join = lambda parts: jnp.concatenate(parts, axis=0)

    gains = jnp.stack([gain_attn, gain_mlp], axis=1)
    gains = jnp.pad(gains, ((0, 0), (0, 126)))
    packed = jnp.concatenate([w_query, w_keyval.reshape(shard_rows, -1), gains], axis=1)
    first = gather_rows(packed)
    qkv_w = first[:, : q_width + 2 * HD]
    gain_pair = first[:, q_width + 2 * HD : q_width + 2 * HD + 2].astype(F32).T
    attn_gain, mlp_gain = gain_pair[0:1], gain_pair[1:2]
    output_w = gather_rows(w_output)
    gateup_w = gather_rows(w_gateup.reshape(shard_rows, 2 * ff))
    down_w = gather_rows(w_down)

    slot_lengths = lax.dynamic_slice_in_dim(lengths, lax.axis_index("dp") * micro, micro)
    slot_of = jnp.repeat(jnp.arange(micro, dtype=jnp.int32), span)
    length_of = jnp.repeat(slot_lengths, span)
    offset = jnp.tile(jnp.arange(span, dtype=jnp.int32), micro)
    position = here * span + offset
    other_position = (1 - here) * span + offset
    live = (position < length_of).astype(F32)[:, None]
    starts = slot_of * SLOT_STEP
    codes = starts + position
    own_codes = jnp.where(position < length_of, codes, NEVER)
    other_codes = jnp.where(other_position < length_of, starts + other_position, NEVER)
    info = jnp.stack([codes, starts])

    frequency = THETA ** (-jnp.arange(0, HD, 2).astype(F32) / HD)
    angles = position.astype(F32)[:, None] * frequency[None, :]
    cosine, sine = jnp.cos(angles), jnp.sin(angles)
    cosine_t, sine_t = cosine.T, sine.T

    hidden_flat = hidden_in.reshape(rows, width)
    seed_flat = cotangent.reshape(rows, width)
    tokens = hidden_flat.astype(F32)

    attn_scale = rms_scale(tokens)
    normed = (tokens * attn_scale * attn_gain).astype(BF16)
    kv_lin = dot(normed, qkv_w[:, q_width:], 1, 0)
    k_low, k_high = kv_lin[:, :half], kv_lin[:, half:HD]
    own_pair = jnp.concatenate(
        [k_low * cosine - k_high * sine, k_high * cosine + k_low * sine, kv_lin[:, HD:]], axis=1
    ).astype(BF16)
    other_pair = lax.ppermute(own_pair, "ctx", [(0, 1), (1, 0)])
    q_lin = dot(qkv_w[:, :q_width], normed, 0, 1).reshape(heads, 2, half, rows) * HD**-0.5
    q_t = jnp.stack(
        [
            q_lin[:, 0] * cosine_t - q_lin[:, 1] * sine_t,
            q_lin[:, 1] * cosine_t + q_lin[:, 0] * sine_t,
        ],
        axis=1,
    ).astype(BF16).reshape(q_width, rows)

    chunk = span // 2
    one, two = slice(0, span), slice(span, 2 * span)
    groups = []
    for at in (one, two):
        pairs = join([own_pair[at], other_pair[at]])
        pairs_t = pairs.T
        key_codes = join([own_codes[at], other_codes[at]])
        groups.append(
            dict(
                flags=block_flags(codes[at], starts[at], key_codes),
                keys=pairs[:, :HD],
                values=pairs[:, HD:],
                keys_t=pairs_t[:HD],
                values_t=pairs_t[HD:],
                codes=key_codes[:, None],
                context=[],
                lse=[],
            )
        )

    def attend_chunk(group, k):
        g = groups[group]
        context, lse = attend(
            g["flags"], q_t, info, g["keys"], g["values_t"], g["codes"], k, group * span // BQ, chunk // BQ
        )
        g["context"].append(context)
        g["lse"].append(lse)
        return dot(context, output_w, 0, 1)

    def push(k, part, size=chunk):
        for n in range(part.shape[0] // size):
            sums.push(k + n, part[n * size : (n + 1) * size].astype(BF16))

    push(0, attend_chunk(0, 0))
    push(1, attend_chunk(0, 1))
    push(2, attend_chunk(1, 0))
    sums.pair(0, (sums.parts[2],))
    push(3, attend_chunk(1, 1))
    sums.pair(1, (sums.parts[3],))
    sums.total(0)
    sums.pair(2)
    sums.total(1)
    sums.pair(3)
    sums.total(2)

    def middle_of(first, at, after=()):
        return sums.ordered(
            middle_fn, sums.of([first, first + 1]), [(hidden_flat, at.start)], [mlp_gain], [BF16, BF16], after=after, name="middle"
        )

    def forward(normed_rows):
        return dot(normed_rows, gateup_w, 1, 0)

    def products(gateup, seed_rows):
        grad_hidden = dot(seed_rows, down_w, 1, 0)
        gate, up = gateup[:, :ff], gateup[:, ff:]
        sigma = jax.nn.sigmoid(gate)
        activated = gate * sigma
        grad_gate = grad_hidden * up * (sigma * (1.0 + gate * (1.0 - sigma)))
        return (activated * up).astype(BF16), jnp.concatenate([grad_gate, grad_hidden * activated], axis=1).astype(BF16)

    mlp_seed = (seed_flat.astype(F32) * live).astype(BF16)
    attn_out_one, normed_one = middle_of(0, one)
    gateup = forward(normed_one)
    sums.total(3, (gateup,))
    hidden_one, grad_gateup_one = products(gateup, mlp_seed[one])
    push(4, dot(grad_gateup_one, gateup_w, 1, 1))
    attn_out_two, normed_two = middle_of(2, two, (sums.parts[5],))
    gateup = forward(normed_two)
    sums.pair(4, (gateup,))
    hidden_two, grad_gateup_two = products(gateup, mlp_seed[two])
    push(6, held_back(dot(grad_gateup_two, gateup_w, 1, 1), sums.last))
    sums.pair(5, (sums.parts[7],))
    sums.total(4)
    hidden = join([hidden_one, hidden_two])
    push(8, held_back(dot(hidden_one, down_w, 1, 1), sums.last), span)
    push(10, held_back(dot(hidden_two, down_w, 1, 1), sums.parts[8]), span)
    sums.pair(6, (sums.parts[10], sums.thirds[4]))
    sums.total(5)
    grad_gateup_w = held_back(
        dot(join([normed_one, normed_two]), join([grad_gateup_one, grad_gateup_two]), 0, 0), sums.last
    ).astype(BF16)
    sums.pair(7, (grad_gateup_w, sums.thirds[5]))
    sums.total(6)
    grad_gateup_w = scatter_rows(once(grad_gateup_w, (sums.totals[6],)))

    def grad_middle_of(first, at, attn_out, after=()):
        return sums.ordered(
            grad_middle_fn,
            sums.of([first, first + 1]),
            [(hidden_flat, at.start), (attn_out, 0), (seed_flat, at.start), (live, at.start)],
            [mlp_gain],
            [F32, BF16],
            sums=1,
            after=after,
            name="grad_middle",
        )

    def attend_back_group(group, seeds):
        g = groups[group]
        grad_context_t = held_back(dot(output_w, seeds, 0, 1), sums.last).astype(BF16)
        carry, grads = None, []
        for k in range(2):
            grad_q, *carry = attend_back(
                g["flags"], q_t, grad_context_t, g["context"][k], g["lse"][k], info, cosine_t, sine_t,
                g["keys"], g["values"], g["keys_t"], g["codes"], k, group * span // BQ, carry,
            )
            grads.append(grad_q)
        returned = lax.ppermute(carry[1], "ctx", [(0, 1), (1, 0)])
        grad_pair = pair_back(carry[0], returned, cosine_t, sine_t, group)
        g["grad"] = jnp.concatenate([jnp.concatenate(grads, axis=1), grad_pair], axis=0)
        return grads[1]

    def attn_back_of(group):
        return dot(groups[group]["grad"], qkv_w, 0, 1)

    grad_middle_one, attn_seed_one, gain_mlp_one = grad_middle_of(4, one, attn_out_one)
    sums.total(7, (sums.thirds[6],))
    done = attend_back_group(0, attn_seed_one)
    sums.pair(8, (done,))
    grad_middle_two, attn_seed_two, gain_mlp_two = grad_middle_of(6, two, attn_out_two)
    push(12, held_back(attn_back_of(0), sums.last))
    done = attend_back_group(1, attn_seed_two)
    sums.pair(10, (done, sums.parts[13]))
    sums.total(8)
    grad_down = held_back(dot(mlp_seed, hidden, 0, 0), sums.last).astype(BF16)
    push(14, held_back(attn_back_of(1), grad_down))
    sums.pair(12, (sums.parts[15],))
    sums.pair(13, (sums.thirds[8],))
    sums.total(10)
    grad_down = scatter_rows(once(grad_down, (sums.totals[10], grad_gateup_w)))
    sums.total(12)
    gain_attn_part = sums.ordered_sum(
        gain_fn, [[sums.parts[12 + k] for k in range(4)]], [(hidden_flat, 0)], "gain_attn"
    )
    extra = jnp.concatenate([fold(gain_attn_part[0], width), fold((gain_mlp_one + gain_mlp_two)[0], width)], axis=1)
    extra = jnp.pad(extra, ((0, 0), (0, 126)))
    grad_qkv_t = jnp.concatenate([groups[0]["grad"], groups[1]["grad"]], axis=1)
    context_t = jnp.concatenate(groups[0]["context"] + groups[1]["context"], axis=1)
    last = jnp.concatenate(
        [
            held_back(dot(normed, grad_qkv_t, 0, 1), sums.last).astype(BF16),
            extra,
            held_back(dot(join([attn_seed_one, attn_seed_two]), context_t, 0, 1), sums.last).astype(BF16),
        ],
        axis=1,
    )

    def result_of(first, at, attn_out, held, after=()):
        return sums.ordered(
            result_fn,
            sums.of([first]),
            [(hidden_flat, at.start), (attn_out, 0), (live, at.start)],
            [],
            [BF16],
            sums=3,
            after=after,
            into=(held, at.start, rows),
            name="result",
        )

    def input_grad_of(first, at, grad_middle, held, after=()):
        return sums.ordered(
            input_grad_fn,
            sums.of([first, first + 1]),
            [(hidden_flat, at.start), (grad_middle, 0)],
            [attn_gain],
            [BF16],
            after=after,
            into=(held, at.start, rows),
            name="input_grad",
        )[0]

    sums.pair(14, (last,))
    sums.total(13)
    sums.pair(15, (sums.thirds[10],))
    sums.total(14)
    sums.total(15, (sums.thirds[12],))
    last = once(last, (sums.totals[15], grad_down))
    last = lax.psum_scatter(last, ROW_AXES, scatter_dimension=0, tiled=True)
    output, *squares_one = result_of(8, one, attn_out_one, None)
    output, *squares_two = result_of(10, two, attn_out_two, output)
    grad_gateup_w = grad_gateup_w.reshape(w_gateup.shape)
    input_grad = input_grad_of(12, one, grad_middle_one, None)
    input_grad = input_grad_of(14, two, grad_middle_two, input_grad, (grad_gateup_w, grad_down))
    last = once(last, (input_grad,)).astype(F32)
    squares = [jnp.sum(x) + jnp.sum(y) for x, y in zip(squares_one, squares_two)]
    squares = spread_small(jnp.broadcast_to(jnp.stack(squares + [0.0])[None, :], (8, 4)))[0, :3]
    root_means = jnp.sqrt(squares / (jnp.sum(lengths).astype(F32) * width))
    at = q_width + 2 * HD
    return (
        output.reshape(hidden_in.shape),
        input_grad.reshape(hidden_in.shape),
        last[:, :q_width],
        last[:, q_width:at].reshape(w_keyval.shape),
        last[:, at + 128 :],
        grad_gateup_w,
        grad_down,
        small_sum(last[:, at]),
        last[:, at + 1],
        root_means,
    )


def solution(mesh):
    placed = (
        P("dp", "ctx", None),
        P(),
        P(("dp", "ctx"), "tensor"),
        P(("dp", "ctx"), "tensor", None),
        P(("dp", "ctx"), "tensor"),
        P(("dp", "ctx"), None, "tensor"),
        P(("dp", "ctx"), "tensor"),
        P(("dp", "ctx")),
        P(("dp", "ctx")),
        P("dp", "ctx", None),
    )
    return jax.shard_map(
        body,
        mesh=mesh,
        in_specs=placed,
        out_specs=(
            P("dp", "ctx", None),
            P("dp", "ctx", None),
            P(("dp", "ctx"), "tensor"),
            P(("dp", "ctx"), "tensor", None),
            P(("dp", "ctx"), "tensor"),
            P(("dp", "ctx"), None, "tensor"),
            P(("dp", "ctx"), "tensor"),
            P(("dp", "ctx")),
            P(("dp", "ctx")),
            P(),
        ),
        check_vma=False,
    )
```
